32 devices in a mesh: groups: 2 (over y), space: 4 (over z), clus: 4 (over x, core).
Axes of the slice: x: 2, y: 2, z: 4, core: 2. Of those that a mesh axis runs over, the one named last changes fastest.
Arguments:
- snapshots: bfloat16 [256, 5, 49152], P('groups', None, ('space', 'clus')), parts along dimension 0
- labels: int32 [256], P('groups'), parts along dimension 0, may hold values from 0 to 3, as said below
- start: float32 [256, 16], P('groups'), parts along dimension 0, may hold values from -6 to 6
- successor: int32 [8], P('groups'), parts along dimension 0, may hold values from 0 to 3, as said below
Outputs:
- modes: bfloat16 [8, 16, 5, 49152], P(('groups', 'clus'), None, None, 'space'), parts along dimension 0
- coefficients: float32 [256, 16], P(('groups', 'clus')), parts along dimension 0
- correlations: float32 [8, 16, 16], P(('groups', 'clus')), parts along dimension 0
The draws below stay inside these ranges and needn't reach their ends.
There are 2 independent parts, one for each index of `groups`. The reference program is written for one: setup_inputs(seed, part) draws one part's arguments, and reference() takes and returns one part's arrays. A program takes and returns all parts, laid end to end along the dimension named above; each array names one. Nothing has to cross between parts.
Inputs may be any that keep to these rules, and one draw needn't show every extreme that they name: `labels`: of the 32 snapshots of each aligned block (those of one index of clus), every cluster holds at least 6 and at most 8; in every block some cluster holds exactly 8. Following successor from any cluster visits all 4 clusters once before returning.
All inputs are finite; a program needn't handle non-finite values.
Results may differ from the reference program's by a relative error of at most 0.0045.
Values may be sent and summed in bfloat16 or wider, within the bound.
No kernel may reach another device: no remote copies, remote signals or barrier semaphores. Data moves between devices by JAX's collectives and lax.ppermute only.
A program may use at most 64 MiB of HBM per device.

```python
import jax
import jax.numpy as jnp
from jax import lax

VARS = 5
MODES = 16
ITERS = 2
SNAP_DEV = 32
K = 4
NSNAP = 128
NCELLS = 49152
CAP = 8
BASE = 6
N_SPACE = 4
N_CLUS = 4


strengths = (0.7, 0.6, 0.55, 0.5, 0.45, 0.4, 0.4, 0.35, 0.35, 0.3, 0.3, 0.25)


def draw_snapshots(key, part):
    keys = jax.random.split(key, 6)
    noise = jax.random.normal(keys[0], (NSNAP, VARS, NCELLS), jnp.float32)
    lagged = jnp.roll(noise, 1, axis=0)
    lag_weight = 0.6 * jax.random.normal(keys[1], (NSNAP, 1, 1), jnp.float32)
    pattern_keys = jax.random.split(keys[2], len(strengths))
    weight_keys = jax.random.split(keys[3], len(strengths))
    shared = jnp.zeros((NSNAP, VARS, NCELLS), jnp.float32)
    for position in range(len(strengths)):
        pattern = jax.random.uniform(pattern_keys[position], (1, VARS, NCELLS), jnp.float32, -1.5, 1.5)
        weight = jax.random.normal(weight_keys[position], (NSNAP, 1, 1), jnp.float32)
        shared = shared + strengths[position] * weight * pattern
    scale = jnp.exp(jax.random.uniform(keys[5], (NSNAP, 1, 1), jnp.float32, -0.5, 0.5))
    values = scale * (noise + lag_weight * lagged + shared)
    return values.astype(jnp.bfloat16)


def draw_labels(key, part):
    blocks = NSNAP // SNAP_DEV
    order = jax.random.permutation(jax.random.fold_in(key, 11), K)
    rest_count = SNAP_DEV - BASE * K - (CAP - BASE)

    def one_block(index):
        block_key = jax.random.fold_in(key, 100 + index)
        pick = jax.random.randint(jax.random.fold_in(block_key, 1), (), 0, max(K // 2, 1))
        hot = order[pick].astype(jnp.int32)
        offset = jax.random.randint(jax.random.fold_in(block_key, 2), (), 0, K - 1)
        base_part = jnp.repeat(jnp.arange(K, dtype=jnp.int32), BASE)
        hot_part = jnp.full((CAP - BASE,), 1, jnp.int32) * hot
        rest_part = (hot + 1 + (jnp.arange(rest_count, dtype=jnp.int32) + offset) % (K - 1)) % K
        joined = jnp.concatenate([base_part, hot_part, rest_part.astype(jnp.int32)])
        shuffle = jax.random.permutation(jax.random.fold_in(block_key, 3), SNAP_DEV)
        return joined[shuffle]
    return jax.vmap(one_block)(jnp.arange(blocks, dtype=jnp.int32)).reshape(NSNAP).astype(jnp.int32)


def draw_successor(key, part):
    order = jax.random.permutation(jax.random.fold_in(key, 5), K).astype(jnp.int32)
    return jnp.zeros((K,), jnp.int32).at[order].set(jnp.roll(order, -1))


def normal_values(rng, shape, scale, most, kind=jnp.bfloat16):
    values = jax.random.normal(rng, shape, jnp.float32) * scale
    return jnp.minimum(jnp.maximum(values, -most), most).astype(kind)


def setup_inputs(seed: int = 0, part: int = 0) -> dict:
    key_list = jax.random.split(jax.random.key(seed), 5)
    part_splits = jax.random.split(jax.random.fold_in(key_list[4], part), 5)
    snapshots = draw_snapshots(jax.random.fold_in(jax.random.fold_in(key_list[4], part), 71), part)
    labels = draw_labels(jax.random.fold_in(jax.random.fold_in(key_list[4], part), 71), part)
    start = normal_values(part_splits[2], (NSNAP, MODES), 1.0, 6.0, jnp.float32)
    successor = draw_successor(jax.random.fold_in(jax.random.fold_in(key_list[4], part), 71), part)
    return dict(snapshots=snapshots, labels=labels, start=start, successor=successor)


def subspace(gram, member, start):
    basis = member[:, :, None] * start[None, :, :]
    for step in range(ITERS):
        image = member[:, :, None] * jnp.einsum('st,ktm->ksm', gram, basis, precision=lax.Precision.HIGHEST) + basis
        inner = jnp.einsum('ksm,ksn->kmn', image, image, precision=lax.Precision.HIGHEST)
        lower = jnp.linalg.cholesky(inner)
        basis = lax.linalg.triangular_solve(lower, image, left_side=False, lower=True, transpose_a=True)
    return basis

def reference(snapshots, labels, start, successor):
    count, variables, cells = snapshots.shape
    blocks = N_SPACE * N_CLUS
    width = cells // blocks
    clusters = N_CLUS

    def block_gram(total, index):
        piece = lax.dynamic_slice_in_dim(snapshots, index * width, width, 2).reshape(count, variables * width).astype(jnp.float32)
        return (total + jnp.dot(piece, piece.T, precision=lax.Precision.HIGHEST), None)
    total, unused = lax.scan(block_gram, jnp.zeros((count, count), jnp.float32), jnp.arange(blocks, dtype=jnp.int32))
    gram = total / (variables * cells)
    member = (labels[None, :] == jnp.arange(clusters, dtype=jnp.int32)[:, None]).astype(jnp.float32)
    basis = subspace(gram, member, start)
    coefficients = basis[labels, jnp.arange(count, dtype=jnp.int32)]
    rounded = basis.astype(jnp.bfloat16)
    wide = rounded.astype(jnp.float32)
    left = jnp.transpose(wide, (0, 2, 1)).reshape(clusters * MODES, count)

    def block_modes(index):
        piece = lax.dynamic_slice_in_dim(snapshots, index * width, width, 2).reshape(count, variables * width).astype(jnp.float32)
        return jnp.dot(left, piece, precision=lax.Precision.HIGHEST).astype(jnp.bfloat16).reshape(clusters, MODES, variables, width)
    stacked = lax.map(block_modes, jnp.arange(blocks, dtype=jnp.int32))
    modes = jnp.transpose(stacked, (1, 2, 3, 0, 4)).reshape(clusters, MODES, variables, cells)
    partner = wide[successor]
    image = jnp.einsum('st,atn->asn', gram, partner, precision=lax.Precision.HIGHEST)
    correlations = jnp.einsum('asm,asn->amn', wide, image, precision=lax.Precision.HIGHEST)
    return (modes, coefficients, correlations)
```

```python
import functools

import jax
import jax.numpy as jnp
from jax import lax
from jax.experimental import pallas as pl
from jax.experimental.pallas import tpu as pltpu
from jax.sharding import PartitionSpec as P

ITERS = 2
HIGH = lax.Precision.HIGHEST
VMEM_LIMIT = 48 * 1024 * 1024


def gram_body(x_ref, gram_ref):
    @pl.when(pl.program_id(0) == 0)
    def _():
        gram_ref[...] = jnp.zeros_like(gram_ref)

    x = x_ref[0]
    gram_ref[...] += lax.dot_general(
        x, x, (((1,), (1,)), ((), ())), preferred_element_type=jnp.float32
    )


def partial_gram(x):
    variables, count, cells = x.shape
    return pl.pallas_call(
        gram_body,
        grid=(variables,),
        in_specs=[pl.BlockSpec((1, count, cells), lambda v: (v, 0, 0))],
        out_specs=pl.BlockSpec((count, count), lambda v: (0, 0)),
        out_shape=jax.ShapeDtypeStruct((count, count), jnp.float32),
        cost_estimate=pl.CostEstimate(
            flops=2 * variables * count * count * cells,
            bytes_accessed=2 * variables * count * cells,
            transcendentals=0,
        ),
        name="gram",
    )(x)


def orthonormal(image, same):
    modes = image.shape[0]
    products = jnp.concatenate([image * image[c : c + 1, :] for c in range(modes)], axis=0)
    inner = jnp.dot(products, same, precision=HIGH, preferred_element_type=jnp.float32)
    columns = [inner[c * modes : (c + 1) * modes] for c in range(modes)]
    row = lax.broadcasted_iota(jnp.int32, image.shape, 0)
    scale = jnp.zeros_like(image)
    for j in range(modes):
        pivot = columns[j][j : j + 1, :]
        scale = jnp.where(row == j, lax.rsqrt(pivot), scale)
        if j + 1 < modes:
            factor = jnp.where(row > j, columns[j] * (1.0 / pivot), 0.0)
            for c in range(j + 1, modes):
                columns[c] = columns[c] - factor * columns[c][j : j + 1, :]
            image = image - factor * image[j : j + 1, :]
    return image * scale


def subspace_body(me_ref, gram_ref, row_ref, column_ref, start_ref, basis_ref, left_ref, *, total_rows, clusters):
    row_labels = row_ref[...]
    same = (column_ref[...] == row_labels).astype(jnp.float32)
    gram = gram_ref[...] * same * (1.0 / total_rows)
    rows = lax.broadcasted_iota(jnp.int32, gram.shape, 0)
    lanes = lax.broadcasted_iota(jnp.int32, gram.shape, 1)
    shifted = gram + (rows == lanes).astype(jnp.float32)
    basis = start_ref[...]
    for step in range(ITERS):
        image = jnp.dot(basis, shifted, precision=HIGH, preferred_element_type=jnp.float32)
        basis = orthonormal(image, same)
    basis_ref[...] = basis
    rounded = basis.astype(jnp.bfloat16).astype(jnp.float32)
    for k in range(clusters):
        left_ref[k] = jnp.where(row_labels == (me_ref[0] ^ k), rounded, 0.0).astype(jnp.bfloat16)


def subspace(me, gram, labels, start, total_rows, clusters):
    modes, count = start.shape
    vmem = pl.BlockSpec(memory_space=pltpu.VMEM)
    return pl.pallas_call(
        functools.partial(subspace_body, total_rows=total_rows, clusters=clusters),
        in_specs=[pl.BlockSpec(memory_space=pltpu.SMEM), vmem, vmem, vmem, vmem],
        out_specs=(vmem, vmem),
        out_shape=(
            jax.ShapeDtypeStruct((modes, count), jnp.float32),
            jax.ShapeDtypeStruct((clusters, modes, count), jnp.bfloat16),
        ),
        name="subspace",
    )(me, gram, labels[None, :], labels[:, None], start)


def small_body(me_ref, successor_ref, gram_ref, row_ref, basis_ref, coefficients_ref, correlations_ref, *, total_rows):
    me = me_ref[0]
    row_labels = row_ref[...]
    basis = basis_ref[...]
    rounded = basis.astype(jnp.bfloat16).astype(jnp.float32)
    mine = jnp.where(row_labels == me, rounded, 0.0)
    other = jnp.where(row_labels == successor_ref[me], rounded, 0.0)
    image = jnp.dot(mine, gram_ref[...], precision=HIGH, preferred_element_type=jnp.float32)
    correlations_ref[0] = lax.dot_general(
        image, other, (((1,), (1,)), ((), ())), precision=HIGH, preferred_element_type=jnp.float32
    ) * (1.0 / total_rows)
    count = basis.shape[1]
    own = coefficients_ref.shape[1]
    coefficients_ref[...] = pltpu.roll(basis, (count - me * own) % count, 1)[:, :own]


def small_outputs(me, successor, gram, labels, basis, total_rows, clusters):
    modes, count = basis.shape
    vmem = pl.BlockSpec(memory_space=pltpu.VMEM)
    smem = pl.BlockSpec(memory_space=pltpu.SMEM)
    return pl.pallas_call(
        functools.partial(small_body, total_rows=total_rows),
        in_specs=[smem, smem, vmem, vmem, vmem],
        out_specs=(vmem, vmem),
        out_shape=(
            jax.ShapeDtypeStruct((modes, count // clusters), jnp.float32),
            jax.ShapeDtypeStruct((1, modes, modes), jnp.float32),
        ),
        name="small",
    )(me, successor, gram, labels[None, :], basis)


def modes_body(left_ref, x_ref, *out_refs, order):
    x = x_ref[0]
    for k, out_ref in zip(order, out_refs):
        out_ref[0] = jnp.dot(left_ref[k], x, preferred_element_type=jnp.float32).astype(jnp.bfloat16)


def local_modes(left, x, order):
    variables, count, cells = x.shape
    clusters, modes, _ = left.shape
    out = jax.ShapeDtypeStruct((variables, modes, cells), jnp.bfloat16)
    return pl.pallas_call(
        functools.partial(modes_body, order=order),
        grid=(variables,),
        in_specs=[
            pl.BlockSpec((clusters, modes, count), lambda v: (0, 0, 0)),
            pl.BlockSpec((1, count, cells), lambda v: (v, 0, 0)),
        ],
        out_specs=[pl.BlockSpec((1, modes, cells), lambda v: (v, 0, 0)) for _ in order],
        out_shape=[out for _ in order],
        cost_estimate=pl.CostEstimate(
            flops=2 * variables * count * cells * modes * len(order),
            bytes_accessed=2 * variables * cells * (count + modes * len(order)),
            transcendentals=0,
        ),
        name="modes",
    )(left, x)


def place_body(me_ref, *refs, order, aliased):
    pieces = refs[aliased : aliased + len(order)]
    out_ref = refs[aliased + len(order)]
    sems = refs[aliased + len(order) + 1]
    cells = pieces[0].shape[2]
    copies = []
    for i, k in enumerate(order):
        at = pl.multiple_of((me_ref[0] ^ k) * cells, 128)
        copy = pltpu.make_async_copy(pieces[i], out_ref.at[:, :, pl.ds(at, cells)], sems.at[i])
        copy.start()
        copies.append(copy)
    for copy in copies:
        copy.wait()


def place(me, out, pieces, order, clusters):
    variables, modes, cells = pieces[0].shape
    anywhere = pl.BlockSpec(memory_space=pl.ANY)
    aliased = 0 if out is None else 1
    operands = ([] if out is None else [out]) + list(pieces)
    return pl.pallas_call(
        functools.partial(place_body, order=order, aliased=aliased),
        in_specs=[pl.BlockSpec(memory_space=pltpu.SMEM)] + [anywhere] * len(operands),
        out_specs=anywhere,
        out_shape=jax.ShapeDtypeStruct((variables, modes, clusters * cells), jnp.bfloat16),
        scratch_shapes=[pltpu.SemaphoreType.DMA((len(order),))],
        input_output_aliases={1: 0} if aliased else {},
        name="place",
    )(me, *operands)


def swap(x, axis, offset):
    size = lax.axis_size(axis)
    return lax.ppermute(x, axis, [(i, i ^ offset) for i in range(size)])


def powers(size):
    return [1 << b for b in range(size.bit_length() - 1)]


def local(snapshots, labels, start, successor):
    count, variables, cells = snapshots.shape
    clusters = lax.axis_size("clus")
    space = lax.axis_size("space")
    me = lax.axis_index("clus").astype(jnp.int32).reshape(1)
    total_rows = variables * cells * space * clusters
    x = jnp.transpose(snapshots, (1, 0, 2))
    gram = partial_gram(x)
    for axis, size in (("clus", clusters), ("space", space)):
        for offset in powers(size):
            gram = gram + swap(gram, axis, offset)
    basis, left = subspace(me, gram, labels, start.T, total_rows, clusters)
    far = list(range(2, clusters))
    sent = local_modes(left, x, far)
    got = [swap(piece, "clus", k) for piece, k in zip(sent, far)]
    own, sibling = local_modes(left, x, [0, 1])
    sibling = swap(sibling, "clus", 1)
    coefficients, correlations = small_outputs(me, successor, gram, labels, basis, total_rows, clusters)
    out = place(me, None, [own, sibling], [0, 1], clusters)
    for piece, k in zip(got, far):
        out = place(me, out, [piece], [k], clusters)
    modes_out = jnp.transpose(out, (1, 0, 2))[None]
    return modes_out, coefficients.T, correlations


def solution(mesh):
    in_specs = (P("groups", None, ("space", "clus")), P("groups"), P("groups", None), P("groups"))
    out_specs = (
        P(("groups", "clus"), None, None, "space"),
        P(("groups", "clus"), None),
        P(("groups", "clus"), None, None),
    )
    return jax.shard_map(local, mesh=mesh, in_specs=in_specs, out_specs=out_specs, check_vma=False)
```

```python
import functools

import jax
import jax.numpy as jnp
from jax import lax
from jax.experimental import pallas as pl
from jax.experimental.pallas import tpu as pltpu
from jax.sharding import PartitionSpec as P

ITERS = 2
CAP = 8
HIGH = lax.Precision.HIGHEST
IN_VMEM = pl.BlockSpec(memory_space=pltpu.VMEM)
IN_SMEM = pl.BlockSpec(memory_space=pltpu.SMEM)
ANYWHERE = pl.BlockSpec(memory_space=pl.ANY)
LIMIT = 20 * 1024 * 1024
LARGE = 46 * 1024 * 1024
EARLY = 1152


def call(body, name, in_specs, outs, *operands, flops=0, scratch=(), aliases=None, out_specs=None, limit=LIMIT):
    return pl.pallas_call(
        body,
        in_specs=in_specs,
        out_specs=out_specs or [IN_VMEM] * len(outs),
        out_shape=outs,
        scratch_shapes=list(scratch),
        input_output_aliases=aliases or {},
        compiler_params=pltpu.CompilerParams(vmem_limit_bytes=limit),
        cost_estimate=pl.CostEstimate(flops=0, bytes_accessed=0, transcendentals=0),
        name=name,
    )(*operands)


def same_cluster(row_labels):
    count = row_labels.shape[1]
    wide = jnp.broadcast_to(row_labels.astype(jnp.float32), (count, count))
    return wide.T == wide


def slot_choice(row_labels, same, cluster, slots):
    count = row_labels.shape[1]
    earlier = lax.broadcasted_iota(jnp.int32, (count, count), 0) < lax.broadcasted_iota(
        jnp.int32, (count, count), 1
    )
    rank = jnp.sum(jnp.where(same & earlier, 1.0, 0.0), axis=0, keepdims=True).astype(jnp.int32)
    wanted = lax.broadcasted_iota(jnp.int32, (slots, count), 0)
    return jnp.where((rank == wanted) & (row_labels == cluster), 1.0, 0.0).astype(jnp.bfloat16)


def gram_body(me_ref, row_ref, x_hbm, gram_ref, x_ref, *refs, far):
    pick_refs = refs[: len(far)]
    sems = refs[len(far)]
    variables = x_ref.shape[0]
    copies = [pltpu.make_async_copy(x_hbm.at[v], x_ref.at[v], sems.at[v]) for v in range(variables)]
    for copy in copies:
        copy.start()
    row_labels = row_ref[...]
    same = same_cluster(row_labels)
    slots, early = pick_refs[0].shape[1:]
    choice = jnp.concatenate(
        [slot_choice(row_labels, same, me_ref[0] ^ k, slots) for k in far], axis=0
    )
    total = None
    for v in range(variables):
        copies[v].wait()
        x = x_ref[v]
        part = lax.dot_general(x, x, (((1,), (1,)), ((), ())), preferred_element_type=jnp.float32)
        total = part if total is None else total + part
        rows = jnp.dot(choice, x[:, :early], preferred_element_type=jnp.float32)
        rows = rows.astype(jnp.bfloat16)
        for i, pick_ref in enumerate(pick_refs):
            pick_ref[v] = rows[i * slots : (i + 1) * slots]
    gram_ref[...] = total


def partial_gram(me, labels, x, far, slots, early):
    variables, count, cells = x.shape
    picked = pltpu.VMEM((variables, slots, early), jnp.bfloat16)
    return call(
        functools.partial(gram_body, far=far),
        "gram",
        [IN_SMEM, IN_VMEM, ANYWHERE],
        [pltpu.VMEM((count, count), jnp.float32), pltpu.VMEM(x.shape, x.dtype)] + [picked for _ in far],
        me,
        labels,
        x,
        scratch=[pltpu.SemaphoreType.DMA((variables,))],
        limit=LARGE,
    )


def orthonormal(image, same):
    modes = image.shape[0]
    products = jnp.concatenate([image * image[c : c + 1, :] for c in range(modes)], axis=0)
    inner = jnp.dot(products, same, precision=HIGH, preferred_element_type=jnp.float32)
    columns = [inner[c * modes : (c + 1) * modes] for c in range(modes)]
    row = lax.broadcasted_iota(jnp.int32, image.shape, 0)
    scale = jnp.zeros_like(image)
    for j in range(modes):
        pivot = columns[j][j : j + 1, :]
        scale = jnp.where(row == j, lax.rsqrt(pivot), scale)
        if j + 1 < modes:
            factor = jnp.where(row > j, columns[j] * (1.0 / pivot), 0.0)
            for c in range(j + 1, modes):
                columns[c] = columns[c] - factor * columns[c][j : j + 1, :]
            image = image - factor * image[j : j + 1, :]
    return image * scale


def subspace_body(
    me_ref, first_ref, second_ref, row_ref, start_ref, gram_ref, basis_ref, left_ref, own_ref, *, total_rows
):
    clusters = left_ref.shape[0]
    row_labels = row_ref[...]
    together = same_cluster(row_labels)
    gram = (first_ref[...] + second_ref[...]) * (1.0 / total_rows)
    gram_ref[...] = gram
    same = together.astype(jnp.float32)
    rows = lax.broadcasted_iota(jnp.int32, gram.shape, 0)
    lanes = lax.broadcasted_iota(jnp.int32, gram.shape, 1)
    shifted = gram * same + (rows == lanes).astype(jnp.float32)
    basis = start_ref[...]
    for step in range(ITERS):
        image = jnp.dot(basis, shifted, precision=HIGH, preferred_element_type=jnp.float32)
        basis = orthonormal(image, same)
    basis_ref[...] = basis
    rounded = basis.astype(jnp.bfloat16).astype(jnp.float32)
    me = me_ref[0]
    for k in range(clusters):
        left_ref[k] = jnp.where(row_labels == (me ^ k), rounded, 0.0).astype(jnp.bfloat16)
    choice = slot_choice(row_labels, together, me, own_ref.shape[1])
    own_ref[...] = lax.dot_general(
        rounded.astype(jnp.bfloat16), choice, (((1,), (1,)), ((), ())), preferred_element_type=jnp.float32
    ).astype(jnp.bfloat16)


def subspace(me, first, second, labels, start, total_rows, clusters, slots):
    modes, count = start.shape
    return call(
        functools.partial(subspace_body, total_rows=total_rows),
        "subspace",
        [IN_SMEM, IN_VMEM, IN_VMEM, IN_VMEM, IN_VMEM],
        [
            pltpu.VMEM((count, count), jnp.float32),
            pltpu.VMEM((modes, count), jnp.float32),
            pltpu.VMEM((clusters, modes, count), jnp.bfloat16),
            pltpu.VMEM((modes, slots), jnp.bfloat16),
        ],
        me,
        first,
        second,
        labels,
        start,
    )


def small_body(me_ref, successor_ref, gram_ref, row_ref, basis_ref, coefficients_ref, correlations_ref):
    me = me_ref[0]
    row_labels = row_ref[...]
    basis = basis_ref[...]
    rounded = basis.astype(jnp.bfloat16).astype(jnp.float32)
    mine = jnp.where(row_labels == me, rounded, 0.0)
    other = jnp.where(row_labels == successor_ref[me], rounded, 0.0)
    image = jnp.dot(mine, gram_ref[...], precision=HIGH, preferred_element_type=jnp.float32)
    correlations_ref[0] = lax.dot_general(
        image, other, (((1,), (1,)), ((), ())), precision=HIGH, preferred_element_type=jnp.float32
    )
    count = basis.shape[1]
    own = coefficients_ref.shape[1]
    coefficients_ref[...] = pltpu.roll(basis, (count - me * own) % count, 1)[:, :own]


def small_outputs(me, successor, gram, labels, basis, clusters):
    modes, count = basis.shape
    return call(
        small_body,
        "small",
        [IN_SMEM, IN_SMEM, IN_VMEM, IN_VMEM, IN_VMEM],
        [
            jax.ShapeDtypeStruct((modes, count // clusters), jnp.float32),
            jax.ShapeDtypeStruct((1, modes, modes), jnp.float32),
        ],
        me,
        successor,
        gram,
        labels,
        basis,
    )


def modes_body(left_ref, x_ref, *out_refs):
    clusters, modes, count = left_ref.shape
    near = left_ref[:2].reshape(2 * modes, count)
    left = left_ref[2:].reshape((clusters - 2) * modes, count)
    begin = x_ref.shape[2] - out_refs[2].shape[2]
    for v in range(x_ref.shape[0]):
        product = jnp.dot(left, x_ref[v, :, begin:], preferred_element_type=jnp.float32)
        product = product.astype(jnp.bfloat16)
        for i, out_ref in enumerate(out_refs[2:]):
            out_ref[v] = product[i * modes : (i + 1) * modes]
        product = jnp.dot(near, x_ref[v], preferred_element_type=jnp.float32)
        product = product.astype(jnp.bfloat16)
        for i, out_ref in enumerate(out_refs[:2]):
            out_ref[v] = product[i * modes : (i + 1) * modes]


def local_modes(left, x, begin):
    variables, count, cells = x.shape
    clusters, modes, _ = left.shape
    near = pltpu.VMEM((variables, modes, cells), jnp.bfloat16)
    late = pltpu.VMEM((variables, modes, cells - begin), jnp.bfloat16)
    return call(
        modes_body,
        "modes",
        [IN_VMEM, IN_VMEM],
        [near, near] + [late] * (clusters - 2),
        left,
        x,
    )


def owner_body(me_ref, own_ref, near_ref, near2_ref, *refs, far):
    rows_refs = refs[: len(far)]
    out_ref = refs[len(far)]
    early_refs = refs[len(far) + 1 : 2 * len(far) + 1]
    sems = refs[2 * len(far) + 1]
    me = me_ref[0]
    cells = near_ref.shape[2]
    copies = []

    def put(source, k):
        at = pl.multiple_of((me ^ k) * cells, 128)
        copy = pltpu.make_async_copy(
            source, out_ref.at[:, :, pl.ds(at, source.shape[2])], sems.at[len(copies)]
        )
        copy.start()
        copies.append(copy)

    put(near_ref, 0)
    put(near2_ref, 1)
    own = own_ref[...]
    for k, rows_ref, early_ref in zip(far, rows_refs, early_refs):
        for v in range(rows_ref.shape[0]):
            early_ref[v] = jnp.dot(own, rows_ref[v], preferred_element_type=jnp.float32).astype(
                jnp.bfloat16
            )
        put(early_ref, k)
    for copy in copies:
        copy.wait()


def owner_modes(me, own, near, rows, far, clusters):
    variables, modes, cells = near[0].shape
    early = rows[0].shape[2]
    scratch = [pltpu.VMEM((variables, modes, early), jnp.bfloat16) for _ in far]
    return call(
        functools.partial(owner_body, far=far),
        "owner",
        [IN_SMEM] + [IN_VMEM] * (3 + len(rows)),
        [jax.ShapeDtypeStruct((variables, modes, clusters * cells), jnp.bfloat16)],
        me,
        own,
        *near,
        *rows,
        scratch=scratch + [pltpu.SemaphoreType.DMA((2 + len(far),))],
        out_specs=[ANYWHERE],
    )[0]


def place_body(me_ref, out_in_ref, piece_ref, out_ref, sem, *, offset, cells):
    late = piece_ref.shape[2]
    at = pl.multiple_of((me_ref[0] ^ offset) * cells + (cells - late), 128)
    copy = pltpu.make_async_copy(piece_ref, out_ref.at[:, :, pl.ds(at, late)], sem)
    copy.start()
    copy.wait()


def place(me, out, piece, offset, clusters):
    return call(
        functools.partial(place_body, offset=offset, cells=out.shape[2] // clusters),
        "place",
        [IN_SMEM, ANYWHERE, IN_VMEM],
        [jax.ShapeDtypeStruct(out.shape, out.dtype)],
        me,
        out,
        piece,
        scratch=[pltpu.SemaphoreType.DMA],
        aliases={1: 0},
        out_specs=[ANYWHERE],
    )[0]


def swap(x, axis, offset):
    size = lax.axis_size(axis)
    return lax.ppermute(x, axis, [(i, i ^ offset) for i in range(size)])


def local(snapshots, labels, start, successor):
    count, variables, cells = snapshots.shape
    clusters = lax.axis_size("clus")
    space = lax.axis_size("space")
    me = lax.axis_index("clus").astype(jnp.int32).reshape(1)
    total_rows = variables * cells * space * clusters
    slots = CAP * clusters
    far = list(range(2, clusters))
    labels = labels[None, :]
    x = jnp.transpose(snapshots, (1, 0, 2))
    gram, x, *picked = partial_gram(me, labels, x, far, slots, EARLY)
    rounds = [("clus", 1 << b) for b in range(1, clusters.bit_length() - 1)]
    links = len(rounds)
    rounds += [("clus", 1)]
    rounds += [("space", 1 << b) for b in range(space.bit_length() - 1)]
    other = None
    for step, (axis, offset) in enumerate(rounds):
        if other is not None:
            gram = gram + other
        other = swap(gram, axis, offset)
        if step == links - 1:
            other, *picked = lax.optimization_barrier((other, *picked))
            rows = [swap(piece, "clus", k) for piece, k in zip(picked, far)]
    gram, basis, left, own = subspace(
        me, gram, other, labels, start.T, total_rows, clusters, slots
    )
    own_piece, sibling, *late = local_modes(left, x, EARLY)
    both = lax.optimization_barrier((*late, *rows, sibling))
    late, rows, sibling = both[: len(far)], both[len(far) : -1], both[-1]
    late = [swap(piece, "clus", k) for piece, k in zip(late, far)]
    near = [own_piece, swap(sibling, "clus", 1)]
    coefficients, correlations = small_outputs(me, successor, gram, labels, basis, clusters)
    out = owner_modes(me, own, near, rows, far, clusters)
    for piece, k in zip(late, far):
        out = place(me, out, piece, k, clusters)
    modes_out = jnp.transpose(out, (1, 0, 2))[None]
    return modes_out, coefficients.T, correlations


def solution(mesh):
    in_specs = (P("groups", None, ("space", "clus")), P("groups"), P("groups", None), P("groups"))
    out_specs = (
        P(("groups", "clus"), None, None, "space"),
        P(("groups", "clus"), None),
        P(("groups", "clus"), None, None),
    )
    return jax.shard_map(local, mesh=mesh, in_specs=in_specs, out_specs=out_specs, check_vma=False)
```

```python
import functools

import jax
import jax.numpy as jnp
from jax import lax
from jax.experimental import pallas as pl
from jax.experimental.pallas import tpu as pltpu
from jax.sharding import PartitionSpec as P

ITERS = 2
CAP = 8
HIGH = lax.Precision.HIGHEST
IN_VMEM = pl.BlockSpec(memory_space=pltpu.VMEM)
IN_SMEM = pl.BlockSpec(memory_space=pltpu.SMEM)
ANYWHERE = pl.BlockSpec(memory_space=pl.ANY)
LIMIT = 20 * 1024 * 1024
LARGE = 46 * 1024 * 1024
EARLY = 1024


def call(body, name, in_specs, outs, *operands, scratch=(), aliases=None, out_specs=None, limit=LIMIT):
    return pl.pallas_call(
        body,
        in_specs=in_specs,
        out_specs=out_specs or [IN_VMEM] * len(outs),
        out_shape=outs,
        scratch_shapes=list(scratch),
        input_output_aliases=aliases or {},
        compiler_params=pltpu.CompilerParams(vmem_limit_bytes=limit),
        cost_estimate=pl.CostEstimate(flops=0, bytes_accessed=0, transcendentals=0),
        name=name,
    )(*operands)


def load_body(after_ref, x_hbm, x_ref, sem):
    copy = pltpu.make_async_copy(x_hbm, x_ref, sem)
    copy.start()
    copy.wait()


def load(after, x):
    return call(
        load_body,
        "load",
        [ANYWHERE, ANYWHERE],
        [pltpu.VMEM(x.shape, x.dtype)],
        after,
        x,
        scratch=[pltpu.SemaphoreType.DMA],
        out_specs=[ANYWHERE],
    )[0]


def same_cluster(row_labels):
    count = row_labels.shape[1]
    wide = jnp.broadcast_to(row_labels.astype(jnp.float32), (count, count))
    return wide.T == wide


def slot_choice(row_labels, same, cluster, slots):
    count = row_labels.shape[1]
    earlier = lax.broadcasted_iota(jnp.int32, (count, count), 0) < lax.broadcasted_iota(
        jnp.int32, (count, count), 1
    )
    rank = jnp.sum(jnp.where(same & earlier, 1.0, 0.0), axis=0, keepdims=True).astype(jnp.int32)
    wanted = lax.broadcasted_iota(jnp.int32, (slots, count), 0)
    return jnp.where((rank == wanted) & (row_labels == cluster), 1.0, 0.0).astype(jnp.bfloat16)


def gram_body(row_hbm, x_hbm, gram_ref, *refs, far):
    pick_refs = refs[: len(far)]
    x_ref, row_ref, sems = refs[len(far) :]
    row_copy = pltpu.make_async_copy(row_hbm, row_ref, sems.at[0])
    x_copy = pltpu.make_async_copy(x_hbm, x_ref, sems.at[1])
    row_copy.start()
    x_copy.start()
    row_copy.wait()
    me = lax.axis_index("clus")
    row_labels = row_ref[...]
    same = same_cluster(row_labels)
    slots, early = pick_refs[0].shape[1:]
    choice = jnp.concatenate(
        [slot_choice(row_labels, same, me ^ k, slots) for k in far], axis=0
    )
    x_copy.wait()
    total = None
    for v in range(x_ref.shape[0]):
        x = x_ref[v]
        part = lax.dot_general(x, x, (((1,), (1,)), ((), ())), preferred_element_type=jnp.float32)
        total = part if total is None else total + part
    gram_ref[...] = total
    for v in range(x_ref.shape[0]):
        rows = jnp.dot(choice, x_ref[v, :, :early], preferred_element_type=jnp.float32)
        rows = rows.astype(jnp.bfloat16)
        for i, pick_ref in enumerate(pick_refs):
            pick_ref[v] = rows[i * slots : (i + 1) * slots]


def partial_gram(labels, x, far, slots, early):
    variables, count, cells = x.shape
    picked = pltpu.VMEM((variables, slots, early), jnp.bfloat16)
    return call(
        functools.partial(gram_body, far=far),
        "gram",
        [ANYWHERE, ANYWHERE],
        [pltpu.VMEM((count, count), jnp.float32)] + [picked for _ in far],
        labels,
        x,
        scratch=[
            pltpu.VMEM(x.shape, x.dtype),
            pltpu.VMEM(labels.shape, labels.dtype),
            pltpu.SemaphoreType.DMA((2,)),
        ],
        limit=LARGE,
    )


def orthonormal(image, same):
    modes = image.shape[0]
    products = jnp.concatenate([image * image[c : c + 1, :] for c in range(modes)], axis=0)
    inner = jnp.dot(products, same, precision=HIGH, preferred_element_type=jnp.float32)
    columns = [inner[c * modes : (c + 1) * modes] for c in range(modes)]
    row = lax.broadcasted_iota(jnp.int32, image.shape, 0)
    scale = jnp.zeros_like(image)
    for j in range(modes):
        pivot = columns[j][j : j + 1, :]
        scale = jnp.where(row == j, lax.rsqrt(pivot), scale)
        if j + 1 < modes:
            factor = jnp.where(row > j, columns[j] * (1.0 / pivot), 0.0)
            for c in range(j + 1, modes):
                columns[c] = columns[c] - factor * columns[c][j : j + 1, :]
            image = image - factor * image[j : j + 1, :]
    return image * scale


def subspace_body(
    first_ref, second_ref, row_ref, start_ref, gram_ref, basis_ref, near_ref, left_ref, own_ref, *, total_rows
):
    row_labels = row_ref[...]
    together = same_cluster(row_labels)
    gram = (first_ref[...] + second_ref[...]) * (1.0 / total_rows)
    gram_ref[...] = gram
    same = together.astype(jnp.float32)
    rows = lax.broadcasted_iota(jnp.int32, gram.shape, 0)
    lanes = lax.broadcasted_iota(jnp.int32, gram.shape, 1)
    shifted = gram * same + (rows == lanes).astype(jnp.float32)
    basis = start_ref[...]
    for step in range(ITERS):
        image = jnp.dot(basis, shifted, precision=HIGH, preferred_element_type=jnp.float32)
        basis = orthonormal(image, same)
    basis_ref[...] = basis
    rounded = basis.astype(jnp.bfloat16).astype(jnp.float32)
    me = lax.axis_index("clus")
    for k in range(2):
        near_ref[k] = jnp.where(row_labels == (me ^ k), rounded, 0.0).astype(jnp.bfloat16)
    for k in range(left_ref.shape[0]):
        left_ref[k] = jnp.where(row_labels == (me ^ (k + 2)), rounded, 0.0).astype(jnp.bfloat16)
    choice = slot_choice(row_labels, together, me, own_ref.shape[1])
    own_ref[...] = lax.dot_general(
        rounded.astype(jnp.bfloat16), choice, (((1,), (1,)), ((), ())), preferred_element_type=jnp.float32
    ).astype(jnp.bfloat16)


def subspace(first, second, labels, start, total_rows, clusters, slots):
    modes, count = start.shape
    return call(
        functools.partial(subspace_body, total_rows=total_rows),
        "subspace",
        [IN_VMEM, IN_VMEM, IN_VMEM, IN_VMEM],
        [
            pltpu.VMEM((count, count), jnp.float32),
            pltpu.VMEM((modes, count), jnp.float32),
            pltpu.VMEM((2, modes, count), jnp.bfloat16),
            pltpu.VMEM((clusters - 2, modes, count), jnp.bfloat16),
            pltpu.VMEM((modes, slots), jnp.bfloat16),
        ],
        first,
        second,
        labels,
        start,
    )


def small_body(me_ref, successor_ref, gram_ref, row_ref, basis_ref, coefficients_ref, correlations_ref):
    me = me_ref[0]
    row_labels = row_ref[...]
    basis = basis_ref[...]
    rounded = basis.astype(jnp.bfloat16).astype(jnp.float32)
    mine = jnp.where(row_labels == me, rounded, 0.0)
    other = jnp.where(row_labels == successor_ref[me], rounded, 0.0)
    image = jnp.dot(mine, gram_ref[...], precision=HIGH, preferred_element_type=jnp.float32)
    correlations_ref[0] = lax.dot_general(
        image, other, (((1,), (1,)), ((), ())), precision=HIGH, preferred_element_type=jnp.float32
    )
    count = basis.shape[1]
    own = coefficients_ref.shape[1]
    coefficients_ref[...] = pltpu.roll(basis, (count - me * own) % count, 1)[:, :own]


def small_outputs(me, successor, gram, labels, basis, clusters):
    modes, count = basis.shape
    return call(
        small_body,
        "small",
        [IN_SMEM, IN_SMEM, IN_VMEM, IN_VMEM, IN_VMEM],
        [
            jax.ShapeDtypeStruct((modes, count // clusters), jnp.float32),
            jax.ShapeDtypeStruct((1, modes, modes), jnp.float32),
        ],
        me,
        successor,
        gram,
        labels,
        basis,
    )


def modes_body(near_ref, far_ref, x_ref, *out_refs):
    modes, count = near_ref.shape[1:]
    begin = x_ref.shape[2] - out_refs[2].shape[2]
    for v in range(x_ref.shape[0]):
        for left_ref, refs, at in ((far_ref, out_refs[2:], begin), (near_ref, out_refs[:2], 0)):
            left = left_ref[...].reshape(len(refs) * modes, count)
            product = jnp.dot(left, x_ref[v, :, at:], preferred_element_type=jnp.float32)
            product = product.astype(jnp.bfloat16)
            for i, out_ref in enumerate(refs):
                out_ref[v] = product[i * modes : (i + 1) * modes]


def local_modes(near, left, x, begin):
    variables, count, cells = x.shape
    number, modes, _ = left.shape
    whole = pltpu.VMEM((variables, modes, cells), jnp.bfloat16)
    late = pltpu.VMEM((variables, modes, cells - begin), jnp.bfloat16)
    return call(
        modes_body, "modes", [IN_VMEM] * 3, [whole, whole] + [late] * number, near, left, x
    )


def owner_body(me_ref, own_ref, near_ref, near2_ref, *refs, far):
    rows_refs = refs[: len(far)]
    out_ref = refs[len(far)]
    early_refs = refs[len(far) + 1 : 2 * len(far) + 1]
    sems = refs[2 * len(far) + 1]
    me = me_ref[0]
    cells = near_ref.shape[2]
    copies = []

    def put(source, k):
        at = pl.multiple_of((me ^ k) * cells, 128)
        copy = pltpu.make_async_copy(
            source, out_ref.at[:, :, pl.ds(at, source.shape[2])], sems.at[len(copies)]
        )
        copy.start()
        copies.append(copy)

    put(near_ref, 0)
    put(near2_ref, 1)
    own = own_ref[...]
    for k, rows_ref, early_ref in zip(far, rows_refs, early_refs):
        for v in range(rows_ref.shape[0]):
            early_ref[v] = jnp.dot(own, rows_ref[v], preferred_element_type=jnp.float32).astype(
                jnp.bfloat16
            )
        put(early_ref, k)
    for copy in copies:
        copy.wait()


def owner_modes(me, own, near, rows, far, clusters):
    variables, modes, cells = near[0].shape
    early = rows[0].shape[2]
    scratch = [pltpu.VMEM((variables, modes, early), jnp.bfloat16) for _ in far]
    return call(
        functools.partial(owner_body, far=far),
        "owner",
        [IN_SMEM] + [IN_VMEM] * (3 + len(rows)),
        [jax.ShapeDtypeStruct((variables, modes, clusters * cells), jnp.bfloat16)],
        me,
        own,
        *near,
        *rows,
        scratch=scratch + [pltpu.SemaphoreType.DMA((2 + len(far),))],
        out_specs=[ANYWHERE],
    )[0]


def place_body(me_ref, out_in_ref, piece_ref, out_ref, sem, *, offset, cells):
    late = piece_ref.shape[2]
    at = pl.multiple_of((me_ref[0] ^ offset) * cells + (cells - late), 128)
    copy = pltpu.make_async_copy(piece_ref, out_ref.at[:, :, pl.ds(at, late)], sem)
    copy.start()
    copy.wait()


def place(me, out, piece, offset, clusters):
    return call(
        functools.partial(place_body, offset=offset, cells=out.shape[2] // clusters),
        "place",
        [IN_SMEM, ANYWHERE, IN_VMEM],
        [jax.ShapeDtypeStruct(out.shape, out.dtype)],
        me,
        out,
        piece,
        scratch=[pltpu.SemaphoreType.DMA],
        aliases={1: 0},
        out_specs=[ANYWHERE],
    )[0]


def swap(x, axis, offset):
    size = lax.axis_size(axis)
    return lax.ppermute(x, axis, [(i, i ^ offset) for i in range(size)])


def local(snapshots, labels, start, successor):
    count, variables, cells = snapshots.shape
    clusters = lax.axis_size("clus")
    space = lax.axis_size("space")
    me = lax.axis_index("clus").astype(jnp.int32).reshape(1)
    total_rows = variables * cells * space * clusters
    slots = CAP * clusters
    far = list(range(2, clusters))
    labels = labels[None, :]
    labels_hbm = pltpu.with_memory_space_constraint(labels, pltpu.HBM)
    x = jnp.transpose(snapshots, (1, 0, 2))
    x_hbm = pltpu.with_memory_space_constraint(x, pltpu.HBM)
    gram, *picked = partial_gram(labels_hbm, x_hbm, far, slots, EARLY)
    terms = [gram] + [swap(gram, "clus", k) for k in range(1, clusters)]
    terms[1], *picked = lax.optimization_barrier((terms[1], *picked))
    rows = [swap(piece, "clus", k) for piece, k in zip(picked, far)]
    while len(terms) > 1:
        terms = [a + b for a, b in zip(terms[::2], terms[1::2])]
    gram = terms[0]
    x = load(gram, x_hbm)
    for b in range(space.bit_length() - 1):
        if b > 0:
            gram = gram + other
        other = swap(gram, "space", 1 << b)
    gram, basis, near, left, own = subspace(
        gram, other, labels, start.T, total_rows, clusters, slots
    )
    own_piece, sibling, *late = local_modes(near, left, x, EARLY)
    both = lax.optimization_barrier((*late, *rows, sibling))
    late, rows, sibling = both[: len(far)], both[len(far) : -1], both[-1]
    late = [swap(piece, "clus", k) for piece, k in zip(late, far)]
    near = [own_piece, swap(sibling, "clus", 1)]
    coefficients, correlations = small_outputs(me, successor, gram, labels, basis, clusters)
    out = owner_modes(me, own, near, rows, far, clusters)
    for piece, k in zip(late, far):
        out = place(me, out, piece, k, clusters)
    modes_out = jnp.transpose(out, (1, 0, 2))[None]
    return modes_out, coefficients.T, correlations


def solution(mesh):
    in_specs = (P("groups", None, ("space", "clus")), P("groups"), P("groups", None), P("groups"))
    out_specs = (
        P(("groups", "clus"), None, None, "space"),
        P(("groups", "clus"), None),
        P(("groups", "clus"), None, None),
    )
    return jax.shard_map(local, mesh=mesh, in_specs=in_specs, out_specs=out_specs, check_vma=False)
```

```python
import functools

import jax
import jax.numpy as jnp
from jax import lax
from jax.experimental import pallas as pl
from jax.experimental.pallas import tpu as pltpu
from jax.sharding import PartitionSpec as P

ITERS = 2
CAP = 8
HIGH = lax.Precision.HIGHEST
IN_VMEM = pl.BlockSpec(memory_space=pltpu.VMEM)
IN_SMEM = pl.BlockSpec(memory_space=pltpu.SMEM)
ANYWHERE = pl.BlockSpec(memory_space=pl.ANY)
LIMIT = 20 * 1024 * 1024
LARGE = 46 * 1024 * 1024
EARLY = 1024


def call(body, name, in_specs, outs, *operands, scratch=(), aliases=None, out_specs=None, limit=LIMIT):
    return pl.pallas_call(
        body,
        in_specs=in_specs,
        out_specs=out_specs or [IN_VMEM] * len(outs),
        out_shape=outs,
        scratch_shapes=list(scratch),
        input_output_aliases=aliases or {},
        compiler_params=pltpu.CompilerParams(vmem_limit_bytes=limit),
        cost_estimate=pl.CostEstimate(flops=0, bytes_accessed=0, transcendentals=0),
        name=name,
    )(*operands)


def load_body(after_ref, x_hbm, x_ref, sem):
    copy = pltpu.make_async_copy(x_hbm, x_ref, sem)
    copy.start()
    copy.wait()


def load(after, x):
    return call(
        load_body,
        "load",
        [ANYWHERE, ANYWHERE],
        [pltpu.VMEM(x.shape, x.dtype)],
        after,
        x,
        scratch=[pltpu.SemaphoreType.DMA],
        out_specs=[ANYWHERE],
    )[0]


def same_cluster(row_labels):
    count = row_labels.shape[1]
    wide = jnp.broadcast_to(row_labels.astype(jnp.float32), (count, count))
    return wide.T == wide


def slot_choice(row_labels, same, cluster, slots):
    count = row_labels.shape[1]
    earlier = lax.broadcasted_iota(jnp.int32, (count, count), 0) < lax.broadcasted_iota(
        jnp.int32, (count, count), 1
    )
    rank = jnp.sum(jnp.where(same & earlier, 1.0, 0.0), axis=0, keepdims=True).astype(jnp.int32)
    wanted = lax.broadcasted_iota(jnp.int32, (slots, count), 0)
    return jnp.where((rank == wanted) & (row_labels == cluster), 1.0, 0.0).astype(jnp.bfloat16)


def pack(gram):
    count = gram.shape[0]
    half = count // 2
    top, bottom = gram[:half], gram[half:]
    row = lax.broadcasted_iota(jnp.int32, top.shape, 0)
    lane = lax.broadcasted_iota(jnp.int32, top.shape, 1)
    top = jnp.where((lane < half) & (row < lane), pltpu.roll(bottom, half, 1), top)
    diagonal = jnp.sum(jnp.where(lane == row + half, bottom, 0.0), axis=0, keepdims=True)
    return jnp.concatenate([top, jnp.broadcast_to(diagonal, (8, count))], axis=0)


def unpack(packed):
    half = packed.shape[0] - 8
    top = packed[:half]
    row = lax.broadcasted_iota(jnp.int32, top.shape, 0)
    lane = lax.broadcasted_iota(jnp.int32, top.shape, 1)
    upper = pltpu.roll(jnp.where((lane < half) & (row < lane), top, 0.0), half, 1)
    upper = jnp.where(lane == row + half, 0.5 * packed[half : half + 1], upper)
    lower = jnp.where(row == lane, 0.5 * top, jnp.where((lane < half) & (row < lane), 0.0, top))
    both = jnp.concatenate([lower, upper], axis=0)
    return both + both.T


def gram_body(row_hbm, x_hbm, gram_ref, *refs, far):
    pick_refs = refs[: len(far)]
    x_ref, row_ref, sems = refs[len(far) :]
    row_copy = pltpu.make_async_copy(row_hbm, row_ref, sems.at[0])
    x_copy = pltpu.make_async_copy(x_hbm, x_ref, sems.at[1])
    row_copy.start()
    x_copy.start()
    row_copy.wait()
    me = lax.axis_index("clus")
    row_labels = row_ref[...]
    same = same_cluster(row_labels)
    slots, early = pick_refs[0].shape[1:]
    choice = jnp.concatenate(
        [slot_choice(row_labels, same, me ^ k, slots) for k in far], axis=0
    )
    x_copy.wait()
    total = None
    for v in range(x_ref.shape[0]):
        x = x_ref[v]
        part = lax.dot_general(x, x, (((1,), (1,)), ((), ())), preferred_element_type=jnp.float32)
        total = part if total is None else total + part
    gram_ref[...] = pack(total)
    for v in range(x_ref.shape[0]):
        rows = jnp.dot(choice, x_ref[v, :, :early], preferred_element_type=jnp.float32)
        rows = rows.astype(jnp.bfloat16)
        for i, pick_ref in enumerate(pick_refs):
            pick_ref[v] = rows[i * slots : (i + 1) * slots]


def partial_gram(labels, x, far, slots, early):
    variables, count, cells = x.shape
    picked = pltpu.VMEM((variables, slots, early), jnp.bfloat16)
    return call(
        functools.partial(gram_body, far=far),
        "gram",
        [ANYWHERE, ANYWHERE],
        [pltpu.VMEM((count // 2 + 8, count), jnp.float32)] + [picked for _ in far],
        labels,
        x,
        scratch=[
            pltpu.VMEM(x.shape, x.dtype),
            pltpu.VMEM(labels.shape, labels.dtype),
            pltpu.SemaphoreType.DMA((2,)),
        ],
        limit=LARGE,
    )


def orthonormal(image, same):
    modes = image.shape[0]
    products = jnp.concatenate([image * image[c : c + 1, :] for c in range(modes)], axis=0)
    inner = jnp.dot(products, same, precision=HIGH, preferred_element_type=jnp.float32)
    columns = [inner[c * modes : (c + 1) * modes] for c in range(modes)]
    row = lax.broadcasted_iota(jnp.int32, image.shape, 0)
    scale = jnp.zeros_like(image)
    for j in range(modes):
        pivot = columns[j][j : j + 1, :]
        scale = jnp.where(row == j, lax.rsqrt(pivot), scale)
        if j + 1 < modes:
            factor = jnp.where(row > j, columns[j] * (1.0 / pivot), 0.0)
            for c in range(j + 1, modes):
                columns[c] = columns[c] - factor * columns[c][j : j + 1, :]
            image = image - factor * image[j : j + 1, :]
    return image * scale


def subspace_body(
    first_ref, second_ref, row_ref, start_ref, gram_ref, basis_ref, near_ref, left_ref, own_ref, *, total_rows
):
    row_labels = row_ref[...]
    together = same_cluster(row_labels)
    gram = unpack(first_ref[...] + second_ref[...]) * (1.0 / total_rows)
    gram_ref[...] = gram
    same = together.astype(jnp.float32)
    rows = lax.broadcasted_iota(jnp.int32, gram.shape, 0)
    lanes = lax.broadcasted_iota(jnp.int32, gram.shape, 1)
    shifted = gram * same + (rows == lanes).astype(jnp.float32)
    basis = start_ref[...]
    for step in range(ITERS):
        image = jnp.dot(basis, shifted, precision=HIGH, preferred_element_type=jnp.float32)
        basis = orthonormal(image, same)
    basis_ref[...] = basis
    rounded = basis.astype(jnp.bfloat16).astype(jnp.float32)
    me = lax.axis_index("clus")
    for k in range(2):
        near_ref[k] = jnp.where(row_labels == (me ^ k), rounded, 0.0).astype(jnp.bfloat16)
    for k in range(left_ref.shape[0]):
        left_ref[k] = jnp.where(row_labels == (me ^ (k + 2)), rounded, 0.0).astype(jnp.bfloat16)
    choice = slot_choice(row_labels, together, me, own_ref.shape[1])
    own_ref[...] = lax.dot_general(
        rounded.astype(jnp.bfloat16), choice, (((1,), (1,)), ((), ())), preferred_element_type=jnp.float32
    ).astype(jnp.bfloat16)


def subspace(first, second, labels, start, total_rows, clusters, slots):
    modes, count = start.shape
    return call(
        functools.partial(subspace_body, total_rows=total_rows),
        "subspace",
        [IN_VMEM, IN_VMEM, IN_VMEM, IN_VMEM],
        [
            pltpu.VMEM((count, count), jnp.float32),
            pltpu.VMEM((modes, count), jnp.float32),
            pltpu.VMEM((2, modes, count), jnp.bfloat16),
            pltpu.VMEM((clusters - 2, modes, count), jnp.bfloat16),
            pltpu.VMEM((modes, slots), jnp.bfloat16),
        ],
        first,
        second,
        labels,
        start,
    )


def small_body(me_ref, successor_ref, gram_ref, row_ref, basis_ref, coefficients_ref, correlations_ref):
    me = me_ref[0]
    row_labels = row_ref[...]
    basis = basis_ref[...]
    rounded = basis.astype(jnp.bfloat16).astype(jnp.float32)
    mine = jnp.where(row_labels == me, rounded, 0.0)
    other = jnp.where(row_labels == successor_ref[me], rounded, 0.0)
    image = jnp.dot(mine, gram_ref[...], precision=HIGH, preferred_element_type=jnp.float32)
    correlations_ref[0] = lax.dot_general(
        image, other, (((1,), (1,)), ((), ())), precision=HIGH, preferred_element_type=jnp.float32
    )
    count = basis.shape[1]
    own = coefficients_ref.shape[1]
    coefficients_ref[...] = pltpu.roll(basis, (count - me * own) % count, 1)[:, :own]


def small_outputs(me, successor, gram, labels, basis, clusters):
    modes, count = basis.shape
    return call(
        small_body,
        "small",
        [IN_SMEM, IN_SMEM, IN_VMEM, IN_VMEM, IN_VMEM],
        [
            jax.ShapeDtypeStruct((modes, count // clusters), jnp.float32),
            jax.ShapeDtypeStruct((1, modes, modes), jnp.float32),
        ],
        me,
        successor,
        gram,
        labels,
        basis,
    )


def modes_body(near_ref, far_ref, x_ref, *out_refs, late_parts, near_parts):
    modes, count = near_ref.shape[1:]
    number = far_ref.shape[0]
    own_ref = out_refs[0]
    sibling_refs = out_refs[1 : 1 + len(near_parts)]
    late_refs = out_refs[1 + len(near_parts) :]
    begin = x_ref.shape[2] - late_refs[0].shape[2]

    def place_of(parts, v):
        part = max(i for i, first in enumerate(parts) if first <= v)
        return part, v - parts[part]

    for v in range(x_ref.shape[0]):
        left = far_ref[...].reshape(number * modes, count)
        product = jnp.dot(left, x_ref[v, :, begin:], preferred_element_type=jnp.float32)
        product = product.astype(jnp.bfloat16)
        part, at = place_of(late_parts, v)
        for i in range(number):
            late_refs[i * len(late_parts) + part][at] = product[i * modes : (i + 1) * modes]
        left = near_ref[...].reshape(2 * modes, count)
        product = jnp.dot(left, x_ref[v], preferred_element_type=jnp.float32)
        product = product.astype(jnp.bfloat16)
        own_ref[v] = product[:modes]
        part, at = place_of(near_parts, v)
        sibling_refs[part][at] = product[modes:]


def lengths(parts, total):
    return [b - a for a, b in zip(parts, list(parts[1:]) + [total])]


def local_modes(near, left, x, begin, late_parts, near_parts):
    variables, count, cells = x.shape
    number, modes, _ = left.shape

    def out(length, width):
        return pltpu.VMEM((length, modes, width), jnp.bfloat16)

    sibling = [out(length, cells) for length in lengths(near_parts, variables)]
    late = [out(length, cells - begin) for length in lengths(late_parts, variables)]
    outs = call(
        functools.partial(modes_body, late_parts=late_parts, near_parts=near_parts),
        "modes",
        [IN_VMEM] * 3,
        [out(variables, cells)] + sibling + late * number,
        near,
        left,
        x,
    )
    first = 1 + len(sibling)
    return outs[0], outs[1:first], outs[first:]


def owner_body(me_ref, own_ref, near_ref, *refs, far, near_parts):
    sibling_refs = refs[: len(near_parts)]
    refs = refs[len(near_parts) :]
    rows_refs = refs[: len(far)]
    out_ref = refs[len(far)]
    early_refs = refs[len(far) + 1 : 2 * len(far) + 1]
    sems = refs[2 * len(far) + 1]
    me = me_ref[0]
    cells = near_ref.shape[2]
    copies = []

    def put(source, k, v):
        at = pl.multiple_of((me ^ k) * cells, 128)
        target = out_ref.at[pl.ds(v, source.shape[0]), :, pl.ds(at, source.shape[2])]
        copy = pltpu.make_async_copy(source, target, sems.at[len(copies)])
        copy.start()
        copies.append(copy)

    put(near_ref, 0, 0)
    for v, sibling_ref in zip(near_parts, sibling_refs):
        put(sibling_ref, 1, v)
    own = own_ref[...]
    for k, rows_ref, early_ref in zip(far, rows_refs, early_refs):
        for v in range(rows_ref.shape[0]):
            early_ref[v] = jnp.dot(own, rows_ref[v], preferred_element_type=jnp.float32).astype(
                jnp.bfloat16
            )
        put(early_ref, k, 0)
    for copy in copies:
        copy.wait()


def owner_modes(me, own, near, sibling, near_parts, rows, far, clusters):
    variables, modes, cells = near.shape
    early = rows[0].shape[2]
    scratch = [pltpu.VMEM((variables, modes, early), jnp.bfloat16) for _ in far]
    return call(
        functools.partial(owner_body, far=far, near_parts=near_parts),
        "owner",
        [IN_SMEM] + [IN_VMEM] * (2 + len(sibling) + len(rows)),
        [jax.ShapeDtypeStruct((variables, modes, clusters * cells), jnp.bfloat16)],
        me,
        own,
        near,
        *sibling,
        *rows,
        scratch=scratch + [pltpu.SemaphoreType.DMA((1 + len(sibling) + len(far),))],
        out_specs=[ANYWHERE],
    )[0]


def place_body(me_ref, out_in_ref, *refs, where, cells):
    piece_refs = refs[: len(where)]
    out_ref, sems = refs[len(where) :]
    copies = []
    for (k, v), piece_ref in zip(where, piece_refs):
        length, _, late = piece_ref.shape
        at = pl.multiple_of((me_ref[0] ^ k) * cells + (cells - late), 128)
        target = out_ref.at[pl.ds(v, length), :, pl.ds(at, late)]
        copies.append(pltpu.make_async_copy(piece_ref, target, sems.at[len(copies)]))
        copies[-1].start()
    for copy in copies:
        copy.wait()


def place(me, out, pieces, where, clusters):
    return call(
        functools.partial(place_body, where=where, cells=out.shape[2] // clusters),
        "place",
        [IN_SMEM, ANYWHERE] + [IN_VMEM] * len(pieces),
        [jax.ShapeDtypeStruct(out.shape, out.dtype)],
        me,
        out,
        *pieces,
        scratch=[pltpu.SemaphoreType.DMA((len(pieces),))],
        aliases={1: 0},
        out_specs=[ANYWHERE],
    )[0]


def swap(x, axis, offset):
    size = lax.axis_size(axis)
    return lax.ppermute(x, axis, [(i, i ^ offset) for i in range(size)])


def local(snapshots, labels, start, successor):
    count, variables, cells = snapshots.shape
    clusters = lax.axis_size("clus")
    space = lax.axis_size("space")
    me = lax.axis_index("clus").astype(jnp.int32).reshape(1)
    total_rows = variables * cells * space * clusters
    slots = CAP * clusters
    far = list(range(2, clusters))
    labels = labels[None, :]
    labels_hbm = pltpu.with_memory_space_constraint(labels, pltpu.HBM)
    x = jnp.transpose(snapshots, (1, 0, 2))
    x_hbm = pltpu.with_memory_space_constraint(x, pltpu.HBM)
    gram, *picked = partial_gram(labels_hbm, x_hbm, far, slots, EARLY)
    terms = [gram] + [swap(gram, "clus", k) for k in range(1, clusters)]
    terms[1], *picked = lax.optimization_barrier((terms[1], *picked))
    rows = [swap(piece, "clus", k) for piece, k in zip(picked, far)]
    while len(terms) > 1:
        terms = [a + b for a, b in zip(terms[::2], terms[1::2])]
    gram = terms[0]
    x = load(gram, x_hbm)
    for b in range(space.bit_length() - 1):
        if b > 0:
            gram = gram + other
        other = swap(gram, "space", 1 << b)
    gram, basis, near, left, own = subspace(
        gram, other, labels, start.T, total_rows, clusters, slots
    )
    late_parts, near_parts = (0,), tuple(range(0, variables, 2))
    own_piece, sibling, late = local_modes(near, left, x, EARLY, late_parts, near_parts)
    where = [(k, v) for k in far for v in late_parts]
    late = list(late)
    both = lax.optimization_barrier((late[-1], *rows))
    late[-1], rows = both[0], both[1:]
    late = [swap(piece, "clus", k) for piece, (k, v) in zip(late, where)]
    sibling = [swap(piece, "clus", 1) for piece in sibling]
    coefficients, correlations = small_outputs(me, successor, gram, labels, basis, clusters)
    out = owner_modes(me, own, own_piece, sibling, near_parts, rows, far, clusters)
    for group in (slice(0, -1), slice(-1, None)):
        out = place(me, out, late[group], where[group], clusters)
    modes_out = jnp.transpose(out, (1, 0, 2))[None]
    return modes_out, coefficients.T, correlations


def solution(mesh):
    in_specs = (P("groups", None, ("space", "clus")), P("groups"), P("groups", None), P("groups"))
    out_specs = (
        P(("groups", "clus"), None, None, "space"),
        P(("groups", "clus"), None),
        P(("groups", "clus"), None, None),
    )
    return jax.shard_map(local, mesh=mesh, in_specs=in_specs, out_specs=out_specs, check_vma=False)
```

```python
import functools

import jax
import jax.numpy as jnp
from jax import lax
from jax.experimental import pallas as pl
from jax.experimental.pallas import tpu as pltpu
from jax.sharding import PartitionSpec as P

ITERS = 2
CAP = 8
HIGH = lax.Precision.HIGHEST
IN_VMEM = pl.BlockSpec(memory_space=pltpu.VMEM)
IN_SMEM = pl.BlockSpec(memory_space=pltpu.SMEM)
ANYWHERE = pl.BlockSpec(memory_space=pl.ANY)
LIMIT = 20 * 1024 * 1024
LARGE = 46 * 1024 * 1024
EARLY = 896


def call(body, name, in_specs, outs, *operands, scratch=(), aliases=None, out_specs=None, limit=LIMIT):
    return pl.pallas_call(
        body,
        in_specs=in_specs,
        out_specs=out_specs or [IN_VMEM] * len(outs),
        out_shape=outs,
        scratch_shapes=list(scratch),
        input_output_aliases=aliases or {},
        compiler_params=pltpu.CompilerParams(vmem_limit_bytes=limit),
        cost_estimate=pl.CostEstimate(flops=0, bytes_accessed=0, transcendentals=0),
        name=name,
    )(*operands)


def load_body(after_ref, x_hbm, x_ref, sem):
    copy = pltpu.make_async_copy(x_hbm, x_ref, sem)
    copy.start()
    copy.wait()


def load(after, x):
    return call(
        load_body,
        "load",
        [ANYWHERE, ANYWHERE],
        [pltpu.VMEM(x.shape, x.dtype)],
        after,
        x,
        scratch=[pltpu.SemaphoreType.DMA],
        out_specs=[ANYWHERE],
    )[0]


def same_cluster(row_labels):
    count = row_labels.shape[1]
    wide = jnp.broadcast_to(row_labels.astype(jnp.float32), (count, count))
    return wide.T == wide


def slot_choice(row_labels, same, cluster, slots):
    count = row_labels.shape[1]
    earlier = lax.broadcasted_iota(jnp.int32, (count, count), 0) < lax.broadcasted_iota(
        jnp.int32, (count, count), 1
    )
    rank = jnp.sum(jnp.where(same & earlier, 1.0, 0.0), axis=0, keepdims=True).astype(jnp.int32)
    wanted = lax.broadcasted_iota(jnp.int32, (slots, count), 0)
    return jnp.where((rank == wanted) & (row_labels == cluster), 1.0, 0.0).astype(jnp.bfloat16)


def pack(gram):
    count = gram.shape[0]
    half = count // 2
    top, bottom = gram[:half], gram[half:]
    row = lax.broadcasted_iota(jnp.int32, top.shape, 0)
    lane = lax.broadcasted_iota(jnp.int32, top.shape, 1)
    top = jnp.where((lane < half) & (row < lane), pltpu.roll(bottom, half, 1), top)
    diagonal = jnp.sum(jnp.where(lane == row + half, bottom, 0.0), axis=0, keepdims=True)
    return jnp.concatenate([top, jnp.broadcast_to(diagonal, (8, count))], axis=0)


def unpack(packed):
    half = packed.shape[0] - 8
    top = packed[:half]
    row = lax.broadcasted_iota(jnp.int32, top.shape, 0)
    lane = lax.broadcasted_iota(jnp.int32, top.shape, 1)
    upper = pltpu.roll(jnp.where((lane < half) & (row < lane), top, 0.0), half, 1)
    upper = jnp.where(lane == row + half, 0.5 * packed[half : half + 1], upper)
    lower = jnp.where(row == lane, 0.5 * top, jnp.where((lane < half) & (row < lane), 0.0, top))
    both = jnp.concatenate([lower, upper], axis=0)
    return both + both.T


def gram_body(row_hbm, x_hbm, gram_ref, *refs, far):
    pick_refs = refs[: len(far)]
    x_ref, row_ref, sems = refs[len(far) :]
    row_copy = pltpu.make_async_copy(row_hbm, row_ref, sems.at[0])
    x_copy = pltpu.make_async_copy(x_hbm, x_ref, sems.at[1])
    row_copy.start()
    x_copy.start()
    row_copy.wait()
    me = lax.axis_index("clus")
    row_labels = row_ref[...]
    same = same_cluster(row_labels)
    slots, early = pick_refs[0].shape[1:]
    choice = jnp.concatenate(
        [slot_choice(row_labels, same, me ^ k, slots) for k in far], axis=0
    )
    x_copy.wait()
    total = None
    for v in range(x_ref.shape[0]):
        x = x_ref[v]
        part = lax.dot_general(x, x, (((1,), (1,)), ((), ())), preferred_element_type=jnp.float32)
        total = part if total is None else total + part
    gram_ref[...] = pack(total)
    for v in range(x_ref.shape[0]):
        rows = jnp.dot(choice, x_ref[v, :, :early], preferred_element_type=jnp.float32)
        rows = rows.astype(jnp.bfloat16)
        for i, pick_ref in enumerate(pick_refs):
            pick_ref[v] = rows[i * slots : (i + 1) * slots]


def partial_gram(labels, x, far, slots, early):
    variables, count, cells = x.shape
    picked = pltpu.VMEM((variables, slots, early), jnp.bfloat16)
    return call(
        functools.partial(gram_body, far=far),
        "gram",
        [ANYWHERE, ANYWHERE],
        [pltpu.VMEM((count // 2 + 8, count), jnp.float32)] + [picked for _ in far],
        labels,
        x,
        scratch=[
            pltpu.VMEM(x.shape, x.dtype),
            pltpu.VMEM(labels.shape, labels.dtype),
            pltpu.SemaphoreType.DMA((2,)),
        ],
        limit=LARGE,
    )


def orthonormal(image, same):
    modes = image.shape[0]
    products = jnp.concatenate([image * image[c : c + 1, :] for c in range(modes)], axis=0)
    inner = jnp.dot(products, same, precision=HIGH, preferred_element_type=jnp.float32)
    columns = [inner[c * modes : (c + 1) * modes] for c in range(modes)]
    row = lax.broadcasted_iota(jnp.int32, image.shape, 0)
    scale = jnp.zeros_like(image)
    for j in range(modes):
        pivot = columns[j][j : j + 1, :]
        scale = jnp.where(row == j, lax.rsqrt(pivot), scale)
        if j + 1 < modes:
            factor = jnp.where(row > j, columns[j] * (1.0 / pivot), 0.0)
            for c in range(j + 1, modes):
                columns[c] = columns[c] - factor * columns[c][j : j + 1, :]
            image = image - factor * image[j : j + 1, :]
    return image * scale


def subspace_body(
    first_ref, second_ref, row_ref, start_ref, x_ref, gram_ref, basis_ref, near_ref, own_ref, *late_refs, total_rows
):
    row_labels = row_ref[...]
    together = same_cluster(row_labels)
    gram = unpack(first_ref[...] + second_ref[...]) * (1.0 / total_rows)
    gram_ref[...] = gram
    same = together.astype(jnp.float32)
    rows = lax.broadcasted_iota(jnp.int32, gram.shape, 0)
    lanes = lax.broadcasted_iota(jnp.int32, gram.shape, 1)
    shifted = gram * same + (rows == lanes).astype(jnp.float32)
    basis = start_ref[...]
    for step in range(ITERS):
        image = jnp.dot(basis, shifted, precision=HIGH, preferred_element_type=jnp.float32)
        basis = orthonormal(image, same)
    basis_ref[...] = basis
    rounded = basis.astype(jnp.bfloat16).astype(jnp.float32)
    me = lax.axis_index("clus")
    for k in range(2):
        near_ref[k] = jnp.where(row_labels == (me ^ k), rounded, 0.0).astype(jnp.bfloat16)
    left = jnp.concatenate(
        [jnp.where(row_labels == (me ^ (k + 2)), rounded, 0.0) for k in range(len(late_refs))], axis=0
    ).astype(jnp.bfloat16)
    begin = x_ref.shape[2] - late_refs[0].shape[2]
    modes = rounded.shape[0]
    for v in range(x_ref.shape[0]):
        product = jnp.dot(left, x_ref[v, :, begin:], preferred_element_type=jnp.float32)
        product = product.astype(jnp.bfloat16)
        for k, late_ref in enumerate(late_refs):
            late_ref[v] = product[k * modes : (k + 1) * modes]
    choice = slot_choice(row_labels, together, me, own_ref.shape[1])
    own_ref[...] = lax.dot_general(
        rounded.astype(jnp.bfloat16), choice, (((1,), (1,)), ((), ())), preferred_element_type=jnp.float32
    ).astype(jnp.bfloat16)


def subspace(first, second, labels, start, x, total_rows, clusters, slots, early):
    modes, count = start.shape
    variables, _, cells = x.shape
    late = pltpu.VMEM((variables, modes, cells - early), jnp.bfloat16)
    gram, basis, near, own, *late = call(
        functools.partial(subspace_body, total_rows=total_rows),
        "subspace",
        [IN_VMEM] * 5,
        [
            pltpu.VMEM((count, count), jnp.float32),
            pltpu.VMEM((modes, count), jnp.float32),
            pltpu.VMEM((2, modes, count), jnp.bfloat16),
            pltpu.VMEM((modes, slots), jnp.bfloat16),
        ]
        + [late] * (clusters - 2),
        first,
        second,
        labels,
        start,
        x,
    )
    return gram, basis, near, own, late


def small_body(successor_ref, gram_ref, row_ref, basis_ref, coefficients_ref, correlations_ref):
    me = lax.axis_index("clus")
    row_labels = row_ref[...]
    basis = basis_ref[...]
    rounded = basis.astype(jnp.bfloat16).astype(jnp.float32)
    mine = jnp.where(row_labels == me, rounded, 0.0)
    other = jnp.where(row_labels == successor_ref[me], rounded, 0.0)
    image = jnp.dot(mine, gram_ref[...], precision=HIGH, preferred_element_type=jnp.float32)
    correlations_ref[0] = lax.dot_general(
        image, other, (((1,), (1,)), ((), ())), precision=HIGH, preferred_element_type=jnp.float32
    )
    count = basis.shape[1]
    own = coefficients_ref.shape[1]
    coefficients_ref[...] = pltpu.roll(basis, (count - me * own) % count, 1)[:, :own]


def small_outputs(successor, gram, labels, basis, clusters):
    modes, count = basis.shape
    return call(
        small_body,
        "small",
        [IN_SMEM, IN_VMEM, IN_VMEM, IN_VMEM],
        [
            jax.ShapeDtypeStruct((modes, count // clusters), jnp.float32),
            jax.ShapeDtypeStruct((1, modes, modes), jnp.float32),
        ],
        successor,
        gram,
        labels,
        basis,
    )


def near_body(near_ref, x_ref, own_ref, *sibling_refs, parts):
    modes, count = near_ref.shape[1:]
    left = near_ref[...].reshape(2 * modes, count)
    for v in range(x_ref.shape[0]):
        product = jnp.dot(left, x_ref[v], preferred_element_type=jnp.float32).astype(jnp.bfloat16)
        own_ref[v] = product[:modes]
        part = max(i for i, first in enumerate(parts) if first <= v)
        sibling_refs[part][v - parts[part]] = product[modes:]


def near_modes(near, x, parts):
    variables, count, cells = x.shape
    modes = near.shape[1]
    lengths = [b - a for a, b in zip(parts, parts[1:] + (variables,))]
    own, *sibling = call(
        functools.partial(near_body, parts=parts),
        "near",
        [IN_VMEM, IN_VMEM],
        [pltpu.VMEM((n, modes, cells), jnp.bfloat16) for n in [variables] + lengths],
        near,
        x,
    )
    return own, sibling


def owner_body(own_ref, near_ref, *refs, far, near_parts):
    sibling_refs = refs[: len(near_parts)]
    refs = refs[len(near_parts) :]
    rows_refs = refs[: len(far)]
    out_ref = refs[len(far)]
    early_refs = refs[len(far) + 1 : 2 * len(far) + 1]
    sems = refs[2 * len(far) + 1]
    me = lax.axis_index("clus")
    cells = near_ref.shape[2]
    copies = []

    def put(source, k, v):
        at = pl.multiple_of((me ^ k) * cells, 128)
        target = out_ref.at[pl.ds(v, source.shape[0]), :, pl.ds(at, source.shape[2])]
        copy = pltpu.make_async_copy(source, target, sems.at[len(copies)])
        copy.start()
        copies.append(copy)

    put(near_ref, 0, 0)
    for v, sibling_ref in zip(near_parts, sibling_refs):
        put(sibling_ref, 1, v)
    own = own_ref[...]
    for k, rows_ref, early_ref in zip(far, rows_refs, early_refs):
        for v in range(rows_ref.shape[0]):
            early_ref[v] = jnp.dot(own, rows_ref[v], preferred_element_type=jnp.float32).astype(
                jnp.bfloat16
            )
        put(early_ref, k, 0)
    for copy in copies:
        copy.wait()


def owner_modes(own, near, sibling, near_parts, rows, far, clusters):
    variables, modes, cells = near.shape
    early = rows[0].shape[2]
    scratch = [pltpu.VMEM((variables, modes, early), jnp.bfloat16) for _ in far]
    return call(
        functools.partial(owner_body, far=far, near_parts=near_parts),
        "owner",
        [IN_VMEM] * (2 + len(sibling) + len(rows)),
        [jax.ShapeDtypeStruct((variables, modes, clusters * cells), jnp.bfloat16)],
        own,
        near,
        *sibling,
        *rows,
        scratch=scratch + [pltpu.SemaphoreType.DMA((1 + len(sibling) + len(far),))],
        out_specs=[ANYWHERE],
    )[0]


def place_body(out_in_ref, *refs, offsets, cells):
    piece_refs = refs[: len(offsets)]
    out_ref, sems = refs[len(offsets) :]
    me = lax.axis_index("clus")
    copies = []
    for k, piece_ref in zip(offsets, piece_refs):
        late = piece_ref.shape[2]
        at = pl.multiple_of((me ^ k) * cells + (cells - late), 128)
        target = out_ref.at[:, :, pl.ds(at, late)]
        copies.append(pltpu.make_async_copy(piece_ref, target, sems.at[len(copies)]))
        copies[-1].start()
    for copy in copies:
        copy.wait()


def place(out, pieces, offsets, clusters):
    return call(
        functools.partial(place_body, offsets=offsets, cells=out.shape[2] // clusters),
        "place",
        [ANYWHERE] + [IN_VMEM] * len(pieces),
        [jax.ShapeDtypeStruct(out.shape, out.dtype)],
        out,
        *pieces,
        scratch=[pltpu.SemaphoreType.DMA((len(pieces),))],
        aliases={0: 0},
        out_specs=[ANYWHERE],
    )[0]


def swap(x, axis, offset):
    size = lax.axis_size(axis)
    return lax.ppermute(x, axis, [(i, i ^ offset) for i in range(size)])


def local(snapshots, labels, start, successor):
    count, variables, cells = snapshots.shape
    clusters = lax.axis_size("clus")
    space = lax.axis_size("space")
    total_rows = variables * cells * space * clusters
    slots = CAP * clusters
    far = list(range(2, clusters))
    labels = labels[None, :]
    labels_hbm = pltpu.with_memory_space_constraint(labels, pltpu.HBM)
    x = jnp.transpose(snapshots, (1, 0, 2))
    x_hbm = pltpu.with_memory_space_constraint(x, pltpu.HBM)
    gram, *picked = partial_gram(labels_hbm, x_hbm, far, slots, EARLY)
    terms = [gram] + [swap(gram, "clus", k) for k in range(1, clusters)]
    terms[1], *picked = lax.optimization_barrier((terms[1], *picked))
    rows = [swap(piece, "clus", k) for piece, k in zip(picked, far)]
    while len(terms) > 1:
        terms = [a + b for a, b in zip(terms[::2], terms[1::2])]
    gram = terms[0]
    x = load(gram, x_hbm)
    for b in range(space.bit_length() - 1):
        if b > 0:
            gram = gram + other
        other = swap(gram, "space", 1 << b)
    gram, basis, near, own, late = subspace(
        gram, other, labels, start.T, x, total_rows, clusters, slots, EARLY
    )
    both = lax.optimization_barrier((late[-1], *rows))
    late[-1], rows = both[0], both[1:]
    late = [swap(piece, "clus", k) for piece, k in zip(late, far)]
    parts = tuple(range(0, variables, 2))
    own_piece, sibling = near_modes(near, load(near, x_hbm), parts)
    sibling = [swap(piece, "clus", 1) for piece in sibling]
    coefficients, correlations = small_outputs(successor, gram, labels, basis, clusters)
    out = owner_modes(own, own_piece, sibling, parts, rows, far, clusters)
    for group in (slice(0, -1), slice(-1, None)):
        out = place(out, late[group], far[group], clusters)
    modes_out = jnp.transpose(out, (1, 0, 2))[None]
    return modes_out, coefficients.T, correlations


def solution(mesh):
    in_specs = (P("groups", None, ("space", "clus")), P("groups"), P("groups", None), P("groups"))
    out_specs = (
        P(("groups", "clus"), None, None, "space"),
        P(("groups", "clus"), None),
        P(("groups", "clus"), None, None),
    )
    return jax.shard_map(local, mesh=mesh, in_specs=in_specs, out_specs=out_specs, check_vma=False)
```

```python
import functools

import jax
import jax.numpy as jnp
from jax import lax
from jax.experimental import pallas as pl
from jax.experimental.pallas import tpu as pltpu
from jax.sharding import PartitionSpec as P

ITERS = 2
CAP = 8
HIGH = lax.Precision.HIGHEST
IN_VMEM = pl.BlockSpec(memory_space=pltpu.VMEM)
IN_SMEM = pl.BlockSpec(memory_space=pltpu.SMEM)
ANYWHERE = pl.BlockSpec(memory_space=pl.ANY)
LIMIT = 20 * 1024 * 1024
LARGE = 46 * 1024 * 1024
EARLY = 896


def call(body, name, in_specs, outs, *operands, scratch=(), aliases=None, out_specs=None, limit=LIMIT):
    return pl.pallas_call(
        body,
        in_specs=in_specs,
        out_specs=out_specs or [IN_VMEM] * len(outs),
        out_shape=outs,
        scratch_shapes=list(scratch),
        input_output_aliases=aliases or {},
        compiler_params=pltpu.CompilerParams(vmem_limit_bytes=limit),
        cost_estimate=pl.CostEstimate(flops=0, bytes_accessed=0, transcendentals=0),
        name=name,
    )(*operands)


def load_body(after_ref, x_hbm, x_ref, sem):
    copy = pltpu.make_async_copy(x_hbm, x_ref, sem)
    copy.start()
    copy.wait()


def load(after, x):
    return call(
        load_body,
        "load",
        [ANYWHERE, ANYWHERE],
        [pltpu.VMEM(x.shape, x.dtype)],
        after,
        x,
        scratch=[pltpu.SemaphoreType.DMA],
        out_specs=[ANYWHERE],
    )[0]


def same_cluster(row_labels):
    count = row_labels.shape[1]
    wide = jnp.broadcast_to(row_labels.astype(jnp.float32), (count, count))
    return wide.T == wide


def slot_choice(row_labels, same, cluster, slots):
    count = row_labels.shape[1]
    earlier = lax.broadcasted_iota(jnp.int32, (count, count), 0) < lax.broadcasted_iota(
        jnp.int32, (count, count), 1
    )
    rank = jnp.sum(jnp.where(same & earlier, 1.0, 0.0), axis=0, keepdims=True).astype(jnp.int32)
    wanted = lax.broadcasted_iota(jnp.int32, (slots, count), 0)
    return jnp.where((rank == wanted) & (row_labels == cluster), 1.0, 0.0).astype(jnp.bfloat16)


def pack(gram):
    count = gram.shape[0]
    half = count // 2
    top, bottom = gram[:half], gram[half:]
    row = lax.broadcasted_iota(jnp.int32, top.shape, 0)
    lane = lax.broadcasted_iota(jnp.int32, top.shape, 1)
    top = jnp.where((lane < half) & (row < lane), pltpu.roll(bottom, half, 1), top)
    diagonal = jnp.sum(jnp.where(lane == row + half, bottom, 0.0), axis=0, keepdims=True)
    return jnp.concatenate([top, jnp.broadcast_to(diagonal, (8, count))], axis=0)


def unpack(packed):
    half = packed.shape[0] - 8
    top = packed[:half]
    row = lax.broadcasted_iota(jnp.int32, top.shape, 0)
    lane = lax.broadcasted_iota(jnp.int32, top.shape, 1)
    upper = pltpu.roll(jnp.where((lane < half) & (row < lane), top, 0.0), half, 1)
    upper = jnp.where(lane == row + half, 0.5 * packed[half : half + 1], upper)
    lower = jnp.where(row == lane, 0.5 * top, jnp.where((lane < half) & (row < lane), 0.0, top))
    both = jnp.concatenate([lower, upper], axis=0)
    return both + both.T


def gram_body(row_hbm, x_hbm, gram_ref, *refs, far):
    pick_refs = refs[: len(far)]
    x_ref, row_ref, sems = refs[len(far) :]
    row_copy = pltpu.make_async_copy(row_hbm, row_ref, sems.at[0])
    x_copy = pltpu.make_async_copy(x_hbm, x_ref, sems.at[1])
    row_copy.start()
    x_copy.start()
    row_copy.wait()
    me = lax.axis_index("clus")
    row_labels = row_ref[...]
    same = same_cluster(row_labels)
    slots, early = pick_refs[0].shape[1:]
    choice = jnp.concatenate(
        [slot_choice(row_labels, same, me ^ k, slots) for k in far], axis=0
    )
    x_copy.wait()
    total = None
    for v in range(x_ref.shape[0]):
        x = x_ref[v]
        part = lax.dot_general(x, x, (((1,), (1,)), ((), ())), preferred_element_type=jnp.float32)
        total = part if total is None else total + part
    gram_ref[...] = pack(total)
    for v in range(x_ref.shape[0]):
        rows = jnp.dot(choice, x_ref[v, :, :early], preferred_element_type=jnp.float32)
        rows = rows.astype(jnp.bfloat16)
        for i, pick_ref in enumerate(pick_refs):
            pick_ref[v] = rows[i * slots : (i + 1) * slots]


def partial_gram(labels, x, far, slots, early):
    variables, count, cells = x.shape
    picked = pltpu.VMEM((variables, slots, early), jnp.bfloat16)
    return call(
        functools.partial(gram_body, far=far),
        "gram",
        [ANYWHERE, ANYWHERE],
        [pltpu.VMEM((count // 2 + 8, count), jnp.float32)] + [picked for _ in far],
        labels,
        x,
        scratch=[
            pltpu.VMEM(x.shape, x.dtype),
            pltpu.VMEM(labels.shape, labels.dtype),
            pltpu.SemaphoreType.DMA((2,)),
        ],
        limit=LARGE,
    )


def orthonormal(image, same):
    modes = image.shape[0]
    products = jnp.concatenate([image * image[c : c + 1, :] for c in range(modes)], axis=0)
    inner = jnp.dot(products, same, precision=HIGH, preferred_element_type=jnp.float32)
    columns = [inner[c * modes : (c + 1) * modes] for c in range(modes)]
    row = lax.broadcasted_iota(jnp.int32, image.shape, 0)
    for j in range(modes):
        scale = lax.rsqrt(columns[j][j : j + 1, :])
        solved = image[j : j + 1, :] * scale
        lower = jnp.where(row > j, columns[j] * scale, 0.0)
        image = jnp.where(row == j, solved, image - lower * solved)
        for c in range(j + 1, modes):
            columns[c] = columns[c] - lower * lower[c : c + 1, :]
    return image


def subspace_body(
    first_ref, second_ref, row_ref, start_ref, x_ref, gram_ref, basis_ref, near_ref, own_ref, *late_refs, total_rows
):
    row_labels = row_ref[...]
    together = same_cluster(row_labels)
    gram = unpack(first_ref[...] + second_ref[...]) * (1.0 / total_rows)
    gram_ref[...] = gram
    same = together.astype(jnp.float32)
    rows = lax.broadcasted_iota(jnp.int32, gram.shape, 0)
    lanes = lax.broadcasted_iota(jnp.int32, gram.shape, 1)
    shifted = gram * same + (rows == lanes).astype(jnp.float32)
    basis = start_ref[...]
    for step in range(ITERS):
        image = jnp.dot(basis, shifted, precision=HIGH, preferred_element_type=jnp.float32)
        basis = orthonormal(image, same)
    basis_ref[...] = basis
    rounded = basis.astype(jnp.bfloat16).astype(jnp.float32)
    me = lax.axis_index("clus")
    for k in range(2):
        near_ref[k] = jnp.where(row_labels == (me ^ k), rounded, 0.0).astype(jnp.bfloat16)
    left = jnp.concatenate(
        [jnp.where(row_labels == (me ^ (k + 2)), rounded, 0.0) for k in range(len(late_refs))], axis=0
    ).astype(jnp.bfloat16)
    begin = x_ref.shape[2] - late_refs[0].shape[2]
    modes = rounded.shape[0]
    for v in range(x_ref.shape[0]):
        product = jnp.dot(left, x_ref[v, :, begin:], preferred_element_type=jnp.float32)
        product = product.astype(jnp.bfloat16)
        for k, late_ref in enumerate(late_refs):
            late_ref[v] = product[k * modes : (k + 1) * modes]
    choice = slot_choice(row_labels, together, me, own_ref.shape[1])
    own_ref[...] = lax.dot_general(
        rounded.astype(jnp.bfloat16), choice, (((1,), (1,)), ((), ())), preferred_element_type=jnp.float32
    ).astype(jnp.bfloat16)


def subspace(first, second, labels, start, x, total_rows, clusters, slots, early):
    modes, count = start.shape
    variables, _, cells = x.shape
    late = pltpu.VMEM((variables, modes, cells - early), jnp.bfloat16)
    gram, basis, near, own, *late = call(
        functools.partial(subspace_body, total_rows=total_rows),
        "subspace",
        [IN_VMEM] * 5,
        [
            pltpu.VMEM((count, count), jnp.float32),
            pltpu.VMEM((modes, count), jnp.float32),
            pltpu.VMEM((2, modes, count), jnp.bfloat16),
            pltpu.VMEM((modes, slots), jnp.bfloat16),
        ]
        + [late] * (clusters - 2),
        first,
        second,
        labels,
        start,
        x,
    )
    return gram, basis, near, own, late


def small_body(successor_ref, gram_ref, row_ref, basis_ref, coefficients_ref, correlations_ref):
    me = lax.axis_index("clus")
    row_labels = row_ref[...]
    basis = basis_ref[...]
    rounded = basis.astype(jnp.bfloat16).astype(jnp.float32)
    mine = jnp.where(row_labels == me, rounded, 0.0)
    other = jnp.where(row_labels == successor_ref[me], rounded, 0.0)
    image = jnp.dot(mine, gram_ref[...], precision=HIGH, preferred_element_type=jnp.float32)
    correlations_ref[0] = lax.dot_general(
        image, other, (((1,), (1,)), ((), ())), precision=HIGH, preferred_element_type=jnp.float32
    )
    count = basis.shape[1]
    own = coefficients_ref.shape[1]
    coefficients_ref[...] = pltpu.roll(basis, (count - me * own) % count, 1)[:, :own]


def small_outputs(successor, gram, labels, basis, clusters):
    modes, count = basis.shape
    return call(
        small_body,
        "small",
        [IN_SMEM, IN_VMEM, IN_VMEM, IN_VMEM],
        [
            jax.ShapeDtypeStruct((modes, count // clusters), jnp.float32),
            jax.ShapeDtypeStruct((1, modes, modes), jnp.float32),
        ],
        successor,
        gram,
        labels,
        basis,
    )


def near_body(near_ref, x_ref, own_ref, *sibling_refs, parts):
    modes, count = near_ref.shape[1:]
    left = near_ref[...].reshape(2 * modes, count)
    for v in range(x_ref.shape[0]):
        product = jnp.dot(left, x_ref[v], preferred_element_type=jnp.float32).astype(jnp.bfloat16)
        own_ref[v] = product[:modes]
        part = max(i for i, first in enumerate(parts) if first <= v)
        sibling_refs[part][v - parts[part]] = product[modes:]


def near_modes(near, x, parts):
    variables, count, cells = x.shape
    modes = near.shape[1]
    lengths = [b - a for a, b in zip(parts, parts[1:] + (variables,))]
    own, *sibling = call(
        functools.partial(near_body, parts=parts),
        "near",
        [IN_VMEM, IN_VMEM],
        [pltpu.VMEM((n, modes, cells), jnp.bfloat16) for n in [variables] + lengths],
        near,
        x,
    )
    return own, sibling


def owner_body(own_ref, near_ref, *refs, far, near_parts):
    sibling_refs = refs[: len(near_parts)]
    refs = refs[len(near_parts) :]
    rows_refs = refs[: len(far)]
    out_ref = refs[len(far)]
    early_refs = refs[len(far) + 1 : 2 * len(far) + 1]
    sems = refs[2 * len(far) + 1]
    me = lax.axis_index("clus")
    cells = near_ref.shape[2]
    copies = []

    def put(source, k, v):
        at = pl.multiple_of((me ^ k) * cells, 128)
        target = out_ref.at[pl.ds(v, source.shape[0]), :, pl.ds(at, source.shape[2])]
        copy = pltpu.make_async_copy(source, target, sems.at[len(copies)])
        copy.start()
        copies.append(copy)

    put(near_ref, 0, 0)
    for v, sibling_ref in zip(near_parts, sibling_refs):
        put(sibling_ref, 1, v)
    own = own_ref[...]
    for k, rows_ref, early_ref in zip(far, rows_refs, early_refs):
        for v in range(rows_ref.shape[0]):
            early_ref[v] = jnp.dot(own, rows_ref[v], preferred_element_type=jnp.float32).astype(
                jnp.bfloat16
            )
        put(early_ref, k, 0)
    for copy in copies:
        copy.wait()


def owner_modes(own, near, sibling, near_parts, rows, far, clusters):
    variables, modes, cells = near.shape
    early = rows[0].shape[2]
    scratch = [pltpu.VMEM((variables, modes, early), jnp.bfloat16) for _ in far]
    return call(
        functools.partial(owner_body, far=far, near_parts=near_parts),
        "owner",
        [IN_VMEM] * (2 + len(sibling) + len(rows)),
        [jax.ShapeDtypeStruct((variables, modes, clusters * cells), jnp.bfloat16)],
        own,
        near,
        *sibling,
        *rows,
        scratch=scratch + [pltpu.SemaphoreType.DMA((1 + len(sibling) + len(far),))],
        out_specs=[ANYWHERE],
    )[0]


def place_body(out_in_ref, *refs, offsets, cells):
    piece_refs = refs[: len(offsets)]
    out_ref, sems = refs[len(offsets) :]
    me = lax.axis_index("clus")
    copies = []
    for k, piece_ref in zip(offsets, piece_refs):
        late = piece_ref.shape[2]
        at = pl.multiple_of((me ^ k) * cells + (cells - late), 128)
        target = out_ref.at[:, :, pl.ds(at, late)]
        copies.append(pltpu.make_async_copy(piece_ref, target, sems.at[len(copies)]))
        copies[-1].start()
    for copy in copies:
        copy.wait()


def place(out, pieces, offsets, clusters):
    return call(
        functools.partial(place_body, offsets=offsets, cells=out.shape[2] // clusters),
        "place",
        [ANYWHERE] + [IN_VMEM] * len(pieces),
        [jax.ShapeDtypeStruct(out.shape, out.dtype)],
        out,
        *pieces,
        scratch=[pltpu.SemaphoreType.DMA((len(pieces),))],
        aliases={0: 0},
        out_specs=[ANYWHERE],
    )[0]


def swap(x, axis, offset):
    size = lax.axis_size(axis)
    return lax.ppermute(x, axis, [(i, i ^ offset) for i in range(size)])


def local(snapshots, labels, start, successor):
    count, variables, cells = snapshots.shape
    clusters = lax.axis_size("clus")
    space = lax.axis_size("space")
    total_rows = variables * cells * space * clusters
    slots = CAP * clusters
    far = list(range(2, clusters))
    labels = labels[None, :]
    labels_hbm = pltpu.with_memory_space_constraint(labels, pltpu.HBM)
    x = jnp.transpose(snapshots, (1, 0, 2))
    x_hbm = pltpu.with_memory_space_constraint(x, pltpu.HBM)
    gram, *picked = partial_gram(labels_hbm, x_hbm, far, slots, EARLY)
    terms = [gram] + [swap(gram, "clus", k) for k in range(1, clusters)]
    terms[1], *picked = lax.optimization_barrier((terms[1], *picked))
    rows = [swap(piece, "clus", k) for piece, k in zip(picked, far)]
    while len(terms) > 1:
        terms = [a + b for a, b in zip(terms[::2], terms[1::2])]
    gram = terms[0]
    x = load(gram, x_hbm)
    for b in range(space.bit_length() - 1):
        if b > 0:
            gram = gram + other
        other = swap(gram, "space", 1 << b)
    gram, basis, near, own, late = subspace(
        gram, other, labels, start.T, x, total_rows, clusters, slots, EARLY
    )
    both = lax.optimization_barrier((late[-1], *rows))
    late[-1], rows = both[0], both[1:]
    late = [swap(piece, "clus", k) for piece, k in zip(late, far)]
    parts = tuple(range(0, variables, 2))
    own_piece, sibling = near_modes(near, load(near, x_hbm), parts)
    sibling = [swap(piece, "clus", 1) for piece in sibling]
    coefficients, correlations = small_outputs(successor, gram, labels, basis, clusters)
    out = owner_modes(own, own_piece, sibling, parts, rows, far, clusters)
    for group in (slice(0, -1), slice(-1, None)):
        out = place(out, late[group], far[group], clusters)
    modes_out = jnp.transpose(out, (1, 0, 2))[None]
    return modes_out, coefficients.T, correlations


def solution(mesh):
    in_specs = (P("groups", None, ("space", "clus")), P("groups"), P("groups", None), P("groups"))
    out_specs = (
        P(("groups", "clus"), None, None, "space"),
        P(("groups", "clus"), None),
        P(("groups", "clus"), None, None),
    )
    return jax.shard_map(local, mesh=mesh, in_specs=in_specs, out_specs=out_specs, check_vma=False)
```

```python
import functools

import jax
import jax.numpy as jnp
from jax import lax
from jax.experimental import pallas as pl
from jax.experimental.pallas import tpu as pltpu
from jax.sharding import PartitionSpec as P

ITERS = 2
CAP = 8
HIGH = lax.Precision.HIGHEST
IN_VMEM = pl.BlockSpec(memory_space=pltpu.VMEM)
IN_SMEM = pl.BlockSpec(memory_space=pltpu.SMEM)
ANYWHERE = pl.BlockSpec(memory_space=pl.ANY)
LIMIT = 20 * 1024 * 1024
LARGE = 46 * 1024 * 1024
EARLY = 896


def call(body, name, in_specs, outs, *operands, scratch=(), aliases=None, out_specs=None, limit=LIMIT):
    return pl.pallas_call(
        body,
        in_specs=in_specs,
        out_specs=out_specs or [IN_VMEM] * len(outs),
        out_shape=outs,
        scratch_shapes=list(scratch),
        input_output_aliases=aliases or {},
        compiler_params=pltpu.CompilerParams(vmem_limit_bytes=limit),
        cost_estimate=pl.CostEstimate(flops=0, bytes_accessed=0, transcendentals=0),
        name=name,
    )(*operands)


def load_body(after_ref, x_hbm, x_ref, sem):
    copy = pltpu.make_async_copy(x_hbm, x_ref, sem)
    copy.start()
    copy.wait()


def load(after, x):
    return call(
        load_body,
        "load",
        [ANYWHERE, ANYWHERE],
        [pltpu.VMEM(x.shape, x.dtype)],
        after,
        x,
        scratch=[pltpu.SemaphoreType.DMA],
        out_specs=[ANYWHERE],
    )[0]


def same_cluster(row_labels):
    count = row_labels.shape[1]
    wide = jnp.broadcast_to(row_labels.astype(jnp.float32), (count, count))
    return wide.T == wide


def slot_choice(row_labels, same, cluster, slots):
    count = row_labels.shape[1]
    earlier = lax.broadcasted_iota(jnp.int32, (count, count), 0) < lax.broadcasted_iota(
        jnp.int32, (count, count), 1
    )
    rank = jnp.sum(jnp.where(same & earlier, 1.0, 0.0), axis=0, keepdims=True).astype(jnp.int32)
    wanted = lax.broadcasted_iota(jnp.int32, (slots, count), 0)
    return jnp.where((rank == wanted) & (row_labels == cluster), 1.0, 0.0).astype(jnp.bfloat16)


def pack(gram):
    count = gram.shape[0]
    half = count // 2
    top, bottom = gram[:half], gram[half:]
    row = lax.broadcasted_iota(jnp.int32, top.shape, 0)
    lane = lax.broadcasted_iota(jnp.int32, top.shape, 1)
    top = jnp.where((lane < half) & (row < lane), pltpu.roll(bottom, half, 1), top)
    diagonal = jnp.sum(jnp.where(lane == row + half, bottom, 0.0), axis=0, keepdims=True)
    return jnp.concatenate([top, jnp.broadcast_to(diagonal, (8, count))], axis=0)


def unpack(packed):
    half = packed.shape[0] - 8
    top = packed[:half]
    row = lax.broadcasted_iota(jnp.int32, top.shape, 0)
    lane = lax.broadcasted_iota(jnp.int32, top.shape, 1)
    upper = pltpu.roll(jnp.where((lane < half) & (row < lane), top, 0.0), half, 1)
    upper = jnp.where(lane == row + half, 0.5 * packed[half : half + 1], upper)
    lower = jnp.where(row == lane, 0.5 * top, jnp.where((lane < half) & (row < lane), 0.0, top))
    both = jnp.concatenate([lower, upper], axis=0)
    return both + both.T


def gram_body(row_hbm, x_hbm, gram_ref, *refs, far):
    pick_refs = refs[: len(far)]
    x_ref, row_ref, sems = refs[len(far) :]
    row_copy = pltpu.make_async_copy(row_hbm, row_ref, sems.at[0])
    x_copy = pltpu.make_async_copy(x_hbm, x_ref, sems.at[1])
    row_copy.start()
    x_copy.start()
    row_copy.wait()
    me = lax.axis_index("clus")
    row_labels = row_ref[...]
    same = same_cluster(row_labels)
    slots, early = pick_refs[0].shape[1:]
    choice = jnp.concatenate(
        [slot_choice(row_labels, same, me ^ k, slots) for k in far], axis=0
    )
    x_copy.wait()
    total = None
    for v in range(x_ref.shape[0]):
        x = x_ref[v]
        part = lax.dot_general(x, x, (((1,), (1,)), ((), ())), preferred_element_type=jnp.float32)
        total = part if total is None else total + part
    gram_ref[...] = pack(total)
    for v in range(x_ref.shape[0]):
        rows = jnp.dot(choice, x_ref[v, :, :early], preferred_element_type=jnp.float32)
        rows = rows.astype(jnp.bfloat16)
        for i, pick_ref in enumerate(pick_refs):
            pick_ref[v] = rows[i * slots : (i + 1) * slots]


def partial_gram(labels, x, far, slots, early):
    variables, count, cells = x.shape
    picked = pltpu.VMEM((variables, slots, early), jnp.bfloat16)
    return call(
        functools.partial(gram_body, far=far),
        "gram",
        [ANYWHERE, ANYWHERE],
        [pltpu.VMEM((count // 2 + 8, count), jnp.float32)] + [picked for _ in far],
        labels,
        x,
        scratch=[
            pltpu.VMEM(x.shape, x.dtype),
            pltpu.VMEM(labels.shape, labels.dtype),
            pltpu.SemaphoreType.DMA((2,)),
        ],
        limit=LARGE,
    )


def orthonormal(image, same):
    modes = image.shape[0]
    firsts = [c // 8 * 8 for c in range(modes)]
    products = jnp.concatenate(
        [image[first:] * image[c : c + 1, :] for c, first in enumerate(firsts)], axis=0
    )
    inner = jnp.dot(products, same, precision=HIGH, preferred_element_type=jnp.float32)
    columns = []
    at = 0
    for first in firsts:
        column = inner[at : at + modes - first]
        at += modes - first
        columns.append(
            jnp.concatenate([jnp.zeros_like(image[:first]), column], axis=0) if first else column
        )
    row = lax.broadcasted_iota(jnp.int32, image.shape, 0)
    for j in range(modes):
        scale = lax.rsqrt(columns[j][j : j + 1, :])
        solved = image[j : j + 1, :] * scale
        lower = jnp.where(row > j, columns[j] * scale, 0.0)
        image = jnp.where(row == j, solved, image - lower * solved)
        for c in range(j + 1, modes):
            columns[c] = columns[c] - lower * lower[c : c + 1, :]
    return image


def subspace_body(
    first_ref, second_ref, row_ref, start_ref, x_ref, gram_ref, basis_ref, near_ref, own_ref, *late_refs, total_rows, far
):
    row_labels = row_ref[...]
    together = same_cluster(row_labels)
    gram = unpack(first_ref[...] + second_ref[...]) * (1.0 / total_rows)
    gram_ref[...] = gram
    same = together.astype(jnp.float32)
    rows = lax.broadcasted_iota(jnp.int32, gram.shape, 0)
    lanes = lax.broadcasted_iota(jnp.int32, gram.shape, 1)
    shifted = gram * same + (rows == lanes).astype(jnp.float32)
    basis = start_ref[...]
    for step in range(ITERS):
        image = jnp.dot(basis, shifted, precision=HIGH, preferred_element_type=jnp.float32)
        basis = orthonormal(image, same)
    basis_ref[...] = basis
    rounded = basis.astype(jnp.bfloat16).astype(jnp.float32)
    me = lax.axis_index("clus")
    for k in range(2):
        near_ref[k] = jnp.where(row_labels == (me ^ k), rounded, 0.0).astype(jnp.bfloat16)
    left = jnp.concatenate(
        [jnp.where(row_labels == (me ^ k), rounded, 0.0) for k in far], axis=0
    ).astype(jnp.bfloat16)
    begin = x_ref.shape[2] - late_refs[0].shape[2]
    modes = rounded.shape[0]
    for v in range(x_ref.shape[0]):
        product = jnp.dot(left, x_ref[v, :, begin:], preferred_element_type=jnp.float32)
        product = product.astype(jnp.bfloat16)
        for k, late_ref in enumerate(late_refs):
            late_ref[v] = product[k * modes : (k + 1) * modes]
    choice = slot_choice(row_labels, together, me, own_ref.shape[1])
    own_ref[...] = lax.dot_general(
        rounded.astype(jnp.bfloat16), choice, (((1,), (1,)), ((), ())), preferred_element_type=jnp.float32
    ).astype(jnp.bfloat16)


def subspace(first, second, labels, start, x, total_rows, far, slots, early):
    modes, count = start.shape
    variables, _, cells = x.shape
    late = pltpu.VMEM((variables, modes, cells - early), jnp.bfloat16)
    gram, basis, near, own, *late = call(
        functools.partial(subspace_body, total_rows=total_rows, far=far),
        "subspace",
        [IN_VMEM] * 5,
        [
            pltpu.VMEM((count, count), jnp.float32),
            pltpu.VMEM((modes, count), jnp.float32),
            pltpu.VMEM((2, modes, count), jnp.bfloat16),
            pltpu.VMEM((modes, slots), jnp.bfloat16),
        ]
        + [late] * len(far),
        first,
        second,
        labels,
        start,
        x,
    )
    return gram, basis, near, own, late


def small_body(successor_ref, gram_ref, row_ref, basis_ref, coefficients_ref, correlations_ref):
    me = lax.axis_index("clus")
    row_labels = row_ref[...]
    basis = basis_ref[...]
    rounded = basis.astype(jnp.bfloat16).astype(jnp.float32)
    mine = jnp.where(row_labels == me, rounded, 0.0)
    other = jnp.where(row_labels == successor_ref[me], rounded, 0.0)
    image = jnp.dot(mine, gram_ref[...], precision=HIGH, preferred_element_type=jnp.float32)
    correlations_ref[0] = lax.dot_general(
        image, other, (((1,), (1,)), ((), ())), precision=HIGH, preferred_element_type=jnp.float32
    )
    count = basis.shape[1]
    own = coefficients_ref.shape[1]
    coefficients_ref[...] = pltpu.roll(basis, (count - me * own) % count, 1)[:, :own]


def small_outputs(successor, gram, labels, basis, clusters):
    modes, count = basis.shape
    return call(
        small_body,
        "small",
        [IN_SMEM, IN_VMEM, IN_VMEM, IN_VMEM],
        [
            jax.ShapeDtypeStruct((modes, count // clusters), jnp.float32),
            jax.ShapeDtypeStruct((1, modes, modes), jnp.float32),
        ],
        successor,
        gram,
        labels,
        basis,
    )


def near_body(near_ref, x_ref, own_ref, *sibling_refs, parts):
    modes, count = near_ref.shape[1:]
    left = near_ref[...].reshape(2 * modes, count)
    for v in range(x_ref.shape[0]):
        product = jnp.dot(left, x_ref[v], preferred_element_type=jnp.float32).astype(jnp.bfloat16)
        own_ref[v] = product[:modes]
        part = max(i for i, first in enumerate(parts) if first <= v)
        sibling_refs[part][v - parts[part]] = product[modes:]


def near_modes(near, x, parts):
    variables, count, cells = x.shape
    modes = near.shape[1]
    lengths = [b - a for a, b in zip(parts, parts[1:] + (variables,))]
    own, *sibling = call(
        functools.partial(near_body, parts=parts),
        "near",
        [IN_VMEM, IN_VMEM],
        [pltpu.VMEM((n, modes, cells), jnp.bfloat16) for n in [variables] + lengths],
        near,
        x,
    )
    return own, sibling


def owner_body(own_ref, near_ref, *refs, far, near_parts):
    sibling_refs = refs[: len(near_parts)]
    refs = refs[len(near_parts) :]
    rows_refs = refs[: len(far)]
    out_ref = refs[len(far)]
    early_refs = refs[len(far) + 1 : 2 * len(far) + 1]
    sems = refs[2 * len(far) + 1]
    me = lax.axis_index("clus")
    cells = near_ref.shape[2]
    copies = []

    def put(source, k, v):
        at = pl.multiple_of((me ^ k) * cells, 128)
        target = out_ref.at[pl.ds(v, source.shape[0]), :, pl.ds(at, source.shape[2])]
        copy = pltpu.make_async_copy(source, target, sems.at[len(copies)])
        copy.start()
        copies.append(copy)

    put(near_ref, 0, 0)
    for v, sibling_ref in zip(near_parts, sibling_refs):
        put(sibling_ref, 1, v)
    own = own_ref[...]
    for k, rows_ref, early_ref in zip(far, rows_refs, early_refs):
        for v in range(rows_ref.shape[0]):
            early_ref[v] = jnp.dot(own, rows_ref[v], preferred_element_type=jnp.float32).astype(
                jnp.bfloat16
            )
        put(early_ref, k, 0)
    for copy in copies:
        copy.wait()


def owner_modes(own, near, sibling, near_parts, rows, far, clusters):
    variables, modes, cells = near.shape
    early = rows[0].shape[2]
    scratch = [pltpu.VMEM((variables, modes, early), jnp.bfloat16) for _ in far]
    return call(
        functools.partial(owner_body, far=far, near_parts=near_parts),
        "owner",
        [IN_VMEM] * (2 + len(sibling) + len(rows)),
        [jax.ShapeDtypeStruct((variables, modes, clusters * cells), jnp.bfloat16)],
        own,
        near,
        *sibling,
        *rows,
        scratch=scratch + [pltpu.SemaphoreType.DMA((1 + len(sibling) + len(far),))],
        out_specs=[ANYWHERE],
    )[0]


def place_body(out_in_ref, *refs, offsets, cells):
    piece_refs = refs[: len(offsets)]
    out_ref, sems = refs[len(offsets) :]
    me = lax.axis_index("clus")
    copies = []
    for k, piece_ref in zip(offsets, piece_refs):
        late = piece_ref.shape[2]
        at = pl.multiple_of((me ^ k) * cells + (cells - late), 128)
        target = out_ref.at[:, :, pl.ds(at, late)]
        copies.append(pltpu.make_async_copy(piece_ref, target, sems.at[len(copies)]))
        copies[-1].start()
    for copy in copies:
        copy.wait()


def place(out, pieces, offsets, clusters):
    return call(
        functools.partial(place_body, offsets=offsets, cells=out.shape[2] // clusters),
        "place",
        [ANYWHERE] + [IN_VMEM] * len(pieces),
        [jax.ShapeDtypeStruct(out.shape, out.dtype)],
        out,
        *pieces,
        scratch=[pltpu.SemaphoreType.DMA((len(pieces),))],
        aliases={0: 0},
        out_specs=[ANYWHERE],
    )[0]


def swap(x, axis, offset):
    size = lax.axis_size(axis)
    return lax.ppermute(x, axis, [(i, i ^ offset) for i in range(size)])


def local(snapshots, labels, start, successor):
    count, variables, cells = snapshots.shape
    clusters = lax.axis_size("clus")
    space = lax.axis_size("space")
    total_rows = variables * cells * space * clusters
    slots = CAP * clusters
    far = list(range(2, clusters))
    labels = labels[None, :]
    labels_hbm = pltpu.with_memory_space_constraint(labels, pltpu.HBM)
    x = jnp.transpose(snapshots, (1, 0, 2))
    x_hbm = pltpu.with_memory_space_constraint(x, pltpu.HBM)
    gram, *picked = partial_gram(labels_hbm, x_hbm, far, slots, EARLY)
    terms = [gram] + [swap(gram, "clus", k) for k in range(1, clusters)]
    terms[1], *picked = lax.optimization_barrier((terms[1], *picked))
    rows = [swap(piece, "clus", k) for piece, k in zip(picked[::-1], far[::-1])][::-1]
    while len(terms) > 1:
        terms = [a + b for a, b in zip(terms[::2], terms[1::2])]
    gram = terms[0]
    x = load(gram, x_hbm)
    for b in range(space.bit_length() - 1):
        if b > 0:
            gram = gram + other
        other = swap(gram, "space", 1 << b)
    gram, basis, near, own, late = subspace(
        gram, other, labels, start.T, x, total_rows, far, slots, EARLY
    )
    both = lax.optimization_barrier((late[-1], *rows[::-1]))
    late[-1], rows = both[0], both[:0:-1]
    late = [swap(piece, "clus", k) for piece, k in zip(late, far)]
    parts = tuple(range(0, variables, 2))
    own_piece, sibling = near_modes(near, load(near, x_hbm), parts)
    sibling = [swap(piece, "clus", 1) for piece in sibling]
    coefficients, correlations = small_outputs(successor, gram, labels, basis, clusters)
    out = owner_modes(own, own_piece, sibling, parts, rows, far, clusters)
    for group in (slice(0, -1), slice(-1, None)):
        out = place(out, late[group], far[group], clusters)
    modes_out = jnp.transpose(out, (1, 0, 2))[None]
    return modes_out, coefficients.T, correlations


def solution(mesh):
    in_specs = (P("groups", None, ("space", "clus")), P("groups"), P("groups", None), P("groups"))
    out_specs = (
        P(("groups", "clus"), None, None, "space"),
        P(("groups", "clus"), None),
        P(("groups", "clus"), None, None),
    )
    return jax.shard_map(local, mesh=mesh, in_specs=in_specs, out_specs=out_specs, check_vma=False)
```

```python
import functools

import jax
import jax.numpy as jnp
from jax import lax
from jax.experimental import pallas as pl
from jax.experimental.pallas import tpu as pltpu
from jax.sharding import PartitionSpec as P

ITERS = 2
CAP = 8
HIGH = lax.Precision.HIGHEST
IN_VMEM = pl.BlockSpec(memory_space=pltpu.VMEM)
IN_SMEM = pl.BlockSpec(memory_space=pltpu.SMEM)
ANYWHERE = pl.BlockSpec(memory_space=pl.ANY)
LIMIT = 20 * 1024 * 1024
LARGE = 46 * 1024 * 1024
EARLY = 896


def call(body, name, in_specs, outs, *operands, scratch=(), aliases=None, out_specs=None, limit=LIMIT):
    return pl.pallas_call(
        body,
        in_specs=in_specs,
        out_specs=out_specs or [IN_VMEM] * len(outs),
        out_shape=outs,
        scratch_shapes=list(scratch),
        input_output_aliases=aliases or {},
        compiler_params=pltpu.CompilerParams(vmem_limit_bytes=limit),
        cost_estimate=pl.CostEstimate(flops=0, bytes_accessed=0, transcendentals=0),
        name=name,
    )(*operands)


def load_body(after_ref, x_hbm, x_ref, sem):
    copy = pltpu.make_async_copy(x_hbm, x_ref, sem)
    copy.start()
    copy.wait()


def load(after, x):
    return call(
        load_body,
        "load",
        [ANYWHERE, ANYWHERE],
        [pltpu.VMEM(x.shape, x.dtype)],
        after,
        x,
        scratch=[pltpu.SemaphoreType.DMA],
        out_specs=[ANYWHERE],
    )[0]


def same_cluster(row_labels):
    count = row_labels.shape[1]
    wide = jnp.broadcast_to(row_labels.astype(jnp.float32), (count, count))
    return wide.T == wide


def slot_choice(row_labels, same, cluster, slots):
    count = row_labels.shape[1]
    earlier = lax.broadcasted_iota(jnp.int32, (count, count), 0) < lax.broadcasted_iota(
        jnp.int32, (count, count), 1
    )
    rank = jnp.sum(jnp.where(same & earlier, 1.0, 0.0), axis=0, keepdims=True).astype(jnp.int32)
    wanted = lax.broadcasted_iota(jnp.int32, (slots, count), 0)
    return jnp.where((rank == wanted) & (row_labels == cluster), 1.0, 0.0).astype(jnp.bfloat16)


def pack(gram):
    count = gram.shape[0]
    half = count // 2
    top, bottom = gram[:half], gram[half:]
    row = lax.broadcasted_iota(jnp.int32, top.shape, 0)
    lane = lax.broadcasted_iota(jnp.int32, top.shape, 1)
    top = jnp.where((lane < half) & (row < lane), pltpu.roll(bottom, half, 1), top)
    diagonal = jnp.sum(jnp.where(lane == row + half, bottom, 0.0), axis=0, keepdims=True)
    return jnp.concatenate([top, jnp.broadcast_to(diagonal, (8, count))], axis=0)


def unpack(packed):
    half = packed.shape[0] - 8
    top = packed[:half]
    row = lax.broadcasted_iota(jnp.int32, top.shape, 0)
    lane = lax.broadcasted_iota(jnp.int32, top.shape, 1)
    upper = pltpu.roll(jnp.where((lane < half) & (row < lane), top, 0.0), half, 1)
    upper = jnp.where(lane == row + half, 0.5 * packed[half : half + 1], upper)
    lower = jnp.where(row == lane, 0.5 * top, jnp.where((lane < half) & (row < lane), 0.0, top))
    both = jnp.concatenate([lower, upper], axis=0)
    return both + both.T


def gram_body(row_hbm, x_hbm, gram_ref, *refs, far):
    pick_refs = refs[: len(far)]
    x_ref, row_ref, sems = refs[len(far) :]
    row_copy = pltpu.make_async_copy(row_hbm, row_ref, sems.at[0])
    x_copy = pltpu.make_async_copy(x_hbm, x_ref, sems.at[1])
    row_copy.start()
    x_copy.start()
    row_copy.wait()
    me = lax.axis_index("clus")
    row_labels = row_ref[...]
    same = same_cluster(row_labels)
    slots, early = pick_refs[0].shape[1:]
    choice = jnp.concatenate(
        [slot_choice(row_labels, same, me ^ k, slots) for k in far], axis=0
    )
    x_copy.wait()
    total = None
    for v in range(x_ref.shape[0]):
        x = x_ref[v]
        part = lax.dot_general(x, x, (((1,), (1,)), ((), ())), preferred_element_type=jnp.float32)
        total = part if total is None else total + part
    gram_ref[...] = pack(total)
    for v in range(x_ref.shape[0]):
        rows = jnp.dot(choice, x_ref[v, :, :early], preferred_element_type=jnp.float32)
        rows = rows.astype(jnp.bfloat16)
        for i, pick_ref in enumerate(pick_refs):
            pick_ref[v] = rows[i * slots : (i + 1) * slots]


def partial_gram(labels, x, far, slots, early):
    variables, count, cells = x.shape
    picked = pltpu.VMEM((variables, slots, early), jnp.bfloat16)
    return call(
        functools.partial(gram_body, far=far),
        "gram",
        [ANYWHERE, ANYWHERE],
        [pltpu.VMEM((count // 2 + 8, count), jnp.float32)] + [picked for _ in far],
        labels,
        x,
        scratch=[
            pltpu.VMEM(x.shape, x.dtype),
            pltpu.VMEM(labels.shape, labels.dtype),
            pltpu.SemaphoreType.DMA((2,)),
        ],
        limit=LARGE,
    )


def orthonormal(image, same):
    modes = image.shape[0]
    firsts = [c // 8 * 8 for c in range(modes)]
    products = jnp.concatenate(
        [image[first:] * image[c : c + 1, :] for c, first in enumerate(firsts)], axis=0
    )
    inner = jnp.dot(products, same, precision=HIGH, preferred_element_type=jnp.float32)
    columns = []
    at = 0
    for first in firsts:
        column = inner[at : at + modes - first]
        at += modes - first
        columns.append(
            jnp.concatenate([jnp.zeros_like(image[:first]), column], axis=0) if first else column
        )
    row = lax.broadcasted_iota(jnp.int32, image.shape, 0)
    for j in range(modes):
        scale = lax.rsqrt(columns[j][j : j + 1, :])
        solved = image[j : j + 1, :] * scale
        lower = jnp.where(row > j, columns[j] * scale, 0.0)
        image = jnp.where(row == j, solved, image - lower * solved)
        for c in range(j + 1, modes):
            columns[c] = columns[c] - lower * lower[c : c + 1, :]
    return image


def subspace_body(
    first_ref, second_ref, row_ref, start_ref, x_ref, gram_ref, basis_ref, near_ref, own_ref, *late_refs, total_rows, far
):
    row_labels = row_ref[...]
    together = same_cluster(row_labels)
    gram = unpack(first_ref[...] + second_ref[...]) * (1.0 / total_rows)
    gram_ref[...] = gram
    same = together.astype(jnp.float32)
    rows = lax.broadcasted_iota(jnp.int32, gram.shape, 0)
    lanes = lax.broadcasted_iota(jnp.int32, gram.shape, 1)
    shifted = gram * same + (rows == lanes).astype(jnp.float32)
    basis = start_ref[...]
    for step in range(ITERS):
        image = jnp.dot(basis, shifted, precision=HIGH, preferred_element_type=jnp.float32)
        basis = orthonormal(image, same)
    basis_ref[...] = basis
    rounded = basis.astype(jnp.bfloat16).astype(jnp.float32)
    me = lax.axis_index("clus")
    for k in range(2):
        near_ref[k] = jnp.where(row_labels == (me ^ k), rounded, 0.0).astype(jnp.bfloat16)
    left = jnp.concatenate(
        [jnp.where(row_labels == (me ^ k), rounded, 0.0) for k in far], axis=0
    ).astype(jnp.bfloat16)
    begin = x_ref.shape[2] - late_refs[0].shape[2]
    modes = rounded.shape[0]
    for v in range(x_ref.shape[0]):
        product = jnp.dot(left, x_ref[v, :, begin:], preferred_element_type=jnp.float32)
        product = product.astype(jnp.bfloat16)
        for k, late_ref in enumerate(late_refs):
            late_ref[v] = product[k * modes : (k + 1) * modes]
    choice = slot_choice(row_labels, together, me, own_ref.shape[1])
    own_ref[...] = lax.dot_general(
        rounded.astype(jnp.bfloat16), choice, (((1,), (1,)), ((), ())), preferred_element_type=jnp.float32
    ).astype(jnp.bfloat16)


def subspace(first, second, labels, start, x, total_rows, far, slots, early):
    modes, count = start.shape
    variables, _, cells = x.shape
    late = pltpu.VMEM((variables, modes, cells - early), jnp.bfloat16)
    gram, basis, near, own, *late = call(
        functools.partial(subspace_body, total_rows=total_rows, far=far),
        "subspace",
        [IN_VMEM] * 5,
        [
            pltpu.VMEM((count, count), jnp.float32),
            pltpu.VMEM((modes, count), jnp.float32),
            pltpu.VMEM((2, modes, count), jnp.bfloat16),
            pltpu.VMEM((modes, slots), jnp.bfloat16),
        ]
        + [late] * len(far),
        first,
        second,
        labels,
        start,
        x,
    )
    return gram, basis, near, own, late


def small_body(successor_ref, gram_ref, row_ref, basis_ref, coefficients_ref, correlations_ref):
    me = lax.axis_index("clus")
    row_labels = row_ref[...]
    basis = basis_ref[...]
    rounded = basis.astype(jnp.bfloat16).astype(jnp.float32)
    mine = jnp.where(row_labels == me, rounded, 0.0)
    other = jnp.where(row_labels == successor_ref[me], rounded, 0.0)
    image = jnp.dot(mine, gram_ref[...], precision=HIGH, preferred_element_type=jnp.float32)
    correlations_ref[0] = lax.dot_general(
        image, other, (((1,), (1,)), ((), ())), precision=HIGH, preferred_element_type=jnp.float32
    )
    count = basis.shape[1]
    own = coefficients_ref.shape[1]
    coefficients_ref[...] = pltpu.roll(basis, (count - me * own) % count, 1)[:, :own]


def small_outputs(successor, gram, labels, basis, clusters):
    modes, count = basis.shape
    return call(
        small_body,
        "small",
        [IN_SMEM, IN_VMEM, IN_VMEM, IN_VMEM],
        [
            jax.ShapeDtypeStruct((modes, count // clusters), jnp.float32),
            jax.ShapeDtypeStruct((1, modes, modes), jnp.float32),
        ],
        successor,
        gram,
        labels,
        basis,
    )


def near_body(near_ref, x_ref, own_ref, *sibling_refs, parts):
    modes, count = near_ref.shape[1:]
    left = near_ref[...].reshape(2 * modes, count)
    for v in range(x_ref.shape[0]):
        product = jnp.dot(left, x_ref[v], preferred_element_type=jnp.float32).astype(jnp.bfloat16)
        own_ref[v] = product[:modes]
        part = max(i for i, first in enumerate(parts) if first <= v)
        sibling_refs[part][v - parts[part]] = product[modes:]


def near_modes(near, x, parts):
    variables, count, cells = x.shape
    modes = near.shape[1]
    lengths = [b - a for a, b in zip(parts, parts[1:] + (variables,))]
    own, *sibling = call(
        functools.partial(near_body, parts=parts),
        "near",
        [IN_VMEM, IN_VMEM],
        [pltpu.VMEM((n, modes, cells), jnp.bfloat16) for n in [variables] + lengths],
        near,
        x,
    )
    return own, sibling


def owner_body(own_ref, near_ref, *refs, far, near_parts):
    sibling_refs = refs[: len(near_parts)]
    refs = refs[len(near_parts) :]
    rows_refs = refs[: len(far)]
    out_ref = refs[len(far)]
    early_refs = refs[len(far) + 1 : 2 * len(far) + 1]
    sems = refs[2 * len(far) + 1]
    me = lax.axis_index("clus")
    cells = near_ref.shape[2]
    copies = []

    def put(source, k, v):
        at = pl.multiple_of((me ^ k) * cells, 128)
        target = out_ref.at[pl.ds(v, source.shape[0]), :, pl.ds(at, source.shape[2])]
        copy = pltpu.make_async_copy(source, target, sems.at[len(copies)])
        copy.start()
        copies.append(copy)

    put(near_ref, 0, 0)
    for v, sibling_ref in zip(near_parts, sibling_refs):
        put(sibling_ref, 1, v)
    own = own_ref[...]
    for k, rows_ref, early_ref in zip(far, rows_refs, early_refs):
        for v in range(rows_ref.shape[0]):
            early_ref[v] = jnp.dot(own, rows_ref[v], preferred_element_type=jnp.float32).astype(
                jnp.bfloat16
            )
        put(early_ref, k, 0)
    for copy in copies:
        copy.wait()


def owner_modes(own, near, sibling, near_parts, rows, far, clusters):
    variables, modes, cells = near.shape
    early = rows[0].shape[2]
    scratch = [pltpu.VMEM((variables, modes, early), jnp.bfloat16) for _ in far]
    return call(
        functools.partial(owner_body, far=far, near_parts=near_parts),
        "owner",
        [IN_VMEM] * (2 + len(sibling) + len(rows)),
        [jax.ShapeDtypeStruct((variables, modes, clusters * cells), jnp.bfloat16)],
        own,
        near,
        *sibling,
        *rows,
        scratch=scratch + [pltpu.SemaphoreType.DMA((1 + len(sibling) + len(far),))],
        out_specs=[ANYWHERE],
    )[0]


def place_body(out_in_ref, *refs, offsets, cells):
    piece_refs = refs[: len(offsets)]
    out_ref, sems = refs[len(offsets) :]
    me = lax.axis_index("clus")
    copies = []
    for k, piece_ref in zip(offsets, piece_refs):
        late = piece_ref.shape[2]
        at = pl.multiple_of((me ^ k) * cells + (cells - late), 128)
        target = out_ref.at[:, :, pl.ds(at, late)]
        copies.append(pltpu.make_async_copy(piece_ref, target, sems.at[len(copies)]))
        copies[-1].start()
    for copy in copies:
        copy.wait()


def place(out, pieces, offsets, clusters):
    return call(
        functools.partial(place_body, offsets=offsets, cells=out.shape[2] // clusters),
        "place",
        [ANYWHERE] + [IN_VMEM] * len(pieces),
        [jax.ShapeDtypeStruct(out.shape, out.dtype)],
        out,
        *pieces,
        scratch=[pltpu.SemaphoreType.DMA((len(pieces),))],
        aliases={0: 0},
        out_specs=[ANYWHERE],
    )[0]


def swap(x, axis, offset):
    size = lax.axis_size(axis)
    return lax.ppermute(x, axis, [(i, i ^ offset) for i in range(size)])


def local(snapshots, labels, start, successor):
    count, variables, cells = snapshots.shape
    clusters = lax.axis_size("clus")
    space = lax.axis_size("space")
    total_rows = variables * cells * space * clusters
    slots = CAP * clusters
    far = list(range(2, clusters))
    labels = labels[None, :]
    labels_hbm = pltpu.with_memory_space_constraint(labels, pltpu.HBM)
    x = jnp.transpose(snapshots, (1, 0, 2))
    x_hbm = pltpu.with_memory_space_constraint(x, pltpu.HBM)
    gram, *picked = partial_gram(labels_hbm, x_hbm, far, slots, EARLY)
    terms = [gram] + [swap(gram, "clus", k) for k in range(1, clusters)]
    terms[1], *picked = lax.optimization_barrier((terms[1], *picked))
    rows = [swap(piece, "clus", k) for piece, k in zip(picked[::-1], far[::-1])][::-1]
    while len(terms) > 1:
        terms = [a + b for a, b in zip(terms[::2], terms[1::2])]
    gram = terms[0]
    x = load(gram, x_hbm)
    terms = [gram] + [swap(gram, "space", k) for k in range(1, space)]
    while len(terms) > 2:
        terms = [a + b for a, b in zip(terms[::2], terms[1::2])]
    gram, other = terms
    gram, basis, near, own, late = subspace(
        gram, other, labels, start.T, x, total_rows, far, slots, EARLY
    )
    both = lax.optimization_barrier((late[-1], *rows[::-1]))
    late[-1], rows = both[0], both[:0:-1]
    late = [swap(piece, "clus", k) for piece, k in zip(late, far)]
    parts = tuple(range(0, variables, 2))
    own_piece, sibling = near_modes(near, load(near, x_hbm), parts)
    sibling = [swap(piece, "clus", 1) for piece in sibling]
    coefficients, correlations = small_outputs(successor, gram, labels, basis, clusters)
    out = owner_modes(own, own_piece, sibling, parts, rows, far, clusters)
    for group in (slice(0, -1), slice(-1, None)):
        out = place(out, late[group], far[group], clusters)
    modes_out = jnp.transpose(out, (1, 0, 2))[None]
    return modes_out, coefficients.T, correlations


def solution(mesh):
    in_specs = (P("groups", None, ("space", "clus")), P("groups"), P("groups", None), P("groups"))
    out_specs = (
        P(("groups", "clus"), None, None, "space"),
        P(("groups", "clus"), None),
        P(("groups", "clus"), None, None),
    )
    return jax.shard_map(local, mesh=mesh, in_specs=in_specs, out_specs=out_specs, check_vma=False)
```
